128 devices in a mesh: cp: 8 (over x_hi, y), grp: 16 (over z, x_lo, core).
Axes of the slice: x: 4 (x_hi: 2, x_lo: 2; x = x_hi * 2 + x_lo), y: 4, z: 4, core: 2. Of those that a mesh axis runs over, the one named last changes fastest.
Arguments:
- queries: bfloat16 [32, 1024, 2048], P('grp', 'cp'), may hold values from -108 to 108
- keys: bfloat16 [32, 1024, 2048], P('grp', 'cp'), may hold values from -4 to 4
- values: bfloat16 [32, 1024, 2048], P('grp', 'cp'), may hold values from -6 to 6
- lengths: int32 [32], P('grp'), may hold values from 256 to 1024
- frame_map: bfloat16 [2048, 2176], replicated, may hold values from -0.125 to 0.125
- proj_weight: bfloat16 [2176, 4096], P('grp', 'cp'), may hold values from -0.125 to 0.125
- head_weight: bfloat16 [4096, 256], P('cp'), may hold values from -0.375 to 0.375
- act_embed: float32 [7, 4096], P(None, 'cp'), may hold values from -0.5 to 0.5
- actions: int32 [32, 7], P('grp'), may hold values from 0 to 255
- action_mask: int32 [32, 7], P('grp'), may hold values 0 or 1
- group_ids: int32 [32], P('grp'), may hold values from 0 to 3
- rewards: float32 [32], P('grp'), may hold values from -6 to 6
Outputs:
- logprobs: float32 [32, 7], P('grp')
- grad_proj: bfloat16 [2176, 4096], P('grp', 'cp')
- grad_head: bfloat16 [4096, 256], P('cp')
The draws below stay inside these ranges and needn't reach their ends.
All inputs are finite; a program needn't handle non-finite values. No bound on the sum of `action_mask` on one device may be relied on, other than what follows from the above.
Results may differ from the reference program's by a relative error of at most 0.018.
Values may be sent and summed in bfloat16 or wider, within the bound.
No kernel may reach another device: no remote copies, remote signals or barrier semaphores. Data moves between devices by JAX's collectives and lax.ppermute only.
A program may use at most 128 MiB of HBM per device.

```python
import math
import jax
import jax.numpy as jnp
from jax import lax

TOK_CP = 128
HEADS = 16
HD = 128
VIS = 2176
HID = 4096
NBINS = 256
NACT = 7
SEQ = 1024
EPISODES = 32
NGROUPS = 4
N_CP = 8


def query_key_pair(key):
    base = jax.random.fold_in(key, 31)
    keys_key, target_key, strength_key = jax.random.split(base, 3)
    key_rows = jnp.clip(jax.random.normal(keys_key, (EPISODES, SEQ, HEADS * HD), jnp.float32), -4.0, 4.0)
    key_heads = key_rows.reshape(EPISODES, SEQ, HEADS, HD)
    targets = jax.random.randint(target_key, (EPISODES, SEQ, HEADS, 1), 0, SEQ)
    pointed = jnp.take_along_axis(key_heads, jnp.broadcast_to(targets, (EPISODES, SEQ, HEADS, HD)), axis=1)
    strength = jnp.exp(jax.random.uniform(strength_key, (EPISODES, SEQ, HEADS, 1), jnp.float32, math.log(2.0), math.log(27.0)))
    query_rows = jnp.clip(strength * pointed, -108.0, 108.0).reshape(EPISODES, SEQ, HEADS * HD)
    return (query_rows, key_rows)


def draw_queries(key, part):
    return query_key_pair(key)[0].astype(jnp.bfloat16)


def draw_keys(key, part):
    return query_key_pair(key)[1].astype(jnp.bfloat16)


def draw_values(key, part):
    base = jax.random.fold_in(key, 59)
    coeff_key, direction_key, noise_key = jax.random.split(base, 3)
    coeff = jnp.clip(jax.random.normal(coeff_key, (EPISODES, SEQ, 1), jnp.float32), -3.0, 3.0)
    direction = jnp.clip(jax.random.normal(direction_key, (EPISODES, 1, HEADS * HD), jnp.float32), -3.0, 3.0)
    noise = 0.8 * jax.random.normal(noise_key, (EPISODES, SEQ, HEADS * HD), jnp.float32)
    return jnp.clip(coeff * direction + noise, -6.0, 6.0).astype(jnp.bfloat16)


def draw_act_embed(key, part):
    base = 0.03 * jnp.clip(jax.random.normal(jax.random.fold_in(key, 47), (NACT, HID), jnp.float32), -5.0, 5.0)
    return base


def with_ends(result, key, least, largest):
    extent = result.shape
    place = [jax.random.randint(jax.random.fold_in(key, axis), (), 0, extent[axis]) for axis in range(len(extent))]
    result = result.at[tuple(place)].set(least)
    longest = extent.index(max(extent))
    place[longest] = (place[longest] + 1) % extent[longest]
    return result.at[tuple(place)].set(largest)


def shard_levels(key, extent, cuts, smallest, largest):
    level, own = 1.0, jax.random.fold_in(key, 6)
    for position, blocks in cuts:
        heights = jnp.exp(jax.random.uniform(jax.random.fold_in(own, position), (blocks,), jnp.float32, smallest / len(cuts), largest / len(cuts)))
        level = level * jnp.repeat(heights, extent[position] // blocks).reshape([-1 if axis == position else 1 for axis in range(len(extent))])
    return level


def bell_draw(own_key, dims, deviation, limit, cuts=(), held_as=jnp.bfloat16):
    values = jax.random.normal(own_key, dims, jnp.float32) * deviation
    if len(cuts) > 0:
        values = shard_levels(own_key, dims, cuts, -0.22, 0.18) * values
    return jnp.clip(values, min=-limit, max=limit).astype(held_as)


def setup_inputs(seed: int = 0) -> dict:
    key_of = jax.random.split(jax.random.key(seed), 13)
    queries = draw_queries(jax.random.fold_in(key_of[12], 71), 0)
    keys = draw_keys(jax.random.fold_in(key_of[12], 71), 0)
    values = draw_values(jax.random.fold_in(key_of[12], 71), 0)
    lengths = with_ends(jax.random.randint(key_of[3], (EPISODES,), TOK_CP * N_CP // 4, TOK_CP * N_CP + 1), jax.random.fold_in(key_of[3], 1), TOK_CP * N_CP // 4, TOK_CP * N_CP).astype(jnp.int32)
    frame_map = bell_draw(key_of[4], (HEADS * HD, VIS), (HEADS * HD) ** -0.5, 0.125)
    proj_weight = bell_draw(key_of[5], (VIS, HID), VIS ** -0.5, 0.125, ((0, 16), (1, 8)))
    head_weight = bell_draw(key_of[6], (HID, NBINS), (HID // 16) ** -0.5, 0.375, ((0, 8),))
    act_embed = draw_act_embed(jax.random.fold_in(key_of[12], 71), 0)
    actions = with_ends(jax.random.randint(key_of[8], (EPISODES, NACT), 0, NBINS), jax.random.fold_in(key_of[8], 1), 0, NBINS - 1).astype(jnp.int32)
    action_mask = with_ends((jax.random.randint(key_of[9], (EPISODES, NACT), 0, 4) < 3).astype(jnp.int32), jax.random.fold_in(key_of[9], 1), 0, 1)
    group_ids = with_ends(jax.random.randint(key_of[10], (EPISODES,), 0, NGROUPS), jax.random.fold_in(key_of[10], 1), 0, NGROUPS - 1).astype(jnp.int32)
    rewards = bell_draw(key_of[11], (EPISODES,), 1.0, 6.0, ((0, 16),), jnp.float32)
    return dict(queries=queries, keys=keys, values=values, lengths=lengths, frame_map=frame_map, proj_weight=proj_weight, head_weight=head_weight, act_embed=act_embed, actions=actions, action_mask=action_mask, group_ids=group_ids, rewards=rewards)


SQRT_HALF = 0.7071067811865476
INV_ROOT_TAU = 0.3989422804014327
NEG_LARGE = -1e+30

def gelu_exact(values_in):
    return 0.5 * values_in * (1.0 + lax.erf(values_in * SQRT_HALF))

def gelu_slope(values_in):
    return 0.5 * (1.0 + lax.erf(values_in * SQRT_HALF)) + values_in * jnp.exp(-0.5 * values_in * values_in) * INV_ROOT_TAU

def attend(query_rows, key_rows, value_rows, length):
    query_heads = query_rows.reshape(SEQ, HEADS, HD).astype(jnp.float32)
    key_heads = key_rows.reshape(SEQ, HEADS, HD).astype(jnp.float32)
    value_heads = value_rows.reshape(SEQ, HEADS, HD).astype(jnp.float32)
    scores = jnp.einsum('ihd,jhd->hij', query_heads, key_heads) / math.sqrt(HD)
    live_keys = jnp.arange(SEQ, dtype=jnp.int32) < length
    scores = jnp.where(live_keys[None, None, :], scores, NEG_LARGE)
    row_max = lax.optimization_barrier(jnp.max(scores, axis=-1, keepdims=True))
    probs = jnp.where(live_keys[None, None, :], jnp.exp(scores - row_max), 0.0)
    row_total = lax.optimization_barrier(jnp.sum(probs, axis=-1))
    weighted = jnp.einsum('hij,jhd->ihd', probs.astype(jnp.bfloat16).astype(jnp.float32), value_heads)
    output = weighted / jnp.transpose(row_total)[:, :, None]
    return output.reshape(SEQ, HEADS * HD).astype(jnp.bfloat16)

def reference(queries, keys, values, lengths, frame_map, proj_weight, head_weight, act_embed, actions, action_mask, group_ids, rewards):
    positions = jnp.arange(SEQ, dtype=jnp.int32)

    def forward(element):
        query_rows, key_rows, value_rows, length = element
        attended = attend(query_rows, key_rows, value_rows, length)
        frames = jnp.dot(attended, frame_map, preferred_element_type=jnp.float32).astype(jnp.bfloat16)
        hidden = gelu_exact(jnp.dot(frames, proj_weight, preferred_element_type=jnp.float32))
        token_mask = (positions < length).astype(jnp.float32)
        pooled = lax.optimization_barrier(jnp.sum(token_mask[:, None] * hidden, axis=0)) / length.astype(jnp.float32)
        return (frames, pooled)
    frames, pooled = lax.map(forward, (queries, keys, values, lengths))
    sum_input = pooled[:, None, :] + act_embed[None, :, :]
    head_input = sum_input.astype(jnp.bfloat16).reshape(EPISODES * NACT, HID)
    logits = jnp.dot(head_input, head_weight, preferred_element_type=jnp.float32)
    log_all = jax.nn.log_softmax(logits, axis=-1)
    bin_ids = jnp.arange(NBINS, dtype=jnp.int32)
    picked = (actions.reshape(-1)[:, None] == bin_ids[None, :]).astype(jnp.float32)
    logprobs = lax.optimization_barrier(jnp.sum(picked * log_all, axis=-1)).reshape(EPISODES, NACT)
    membership = (group_ids[:, None] == jnp.arange(NGROUPS, dtype=jnp.int32)[None, :]).astype(jnp.float32)
    group_sizes = lax.optimization_barrier(jnp.sum(membership, axis=0))
    reward_sums = lax.optimization_barrier(jnp.sum(membership * rewards[:, None], axis=0))
    squares = lax.optimization_barrier(jnp.sum(membership * (rewards * rewards)[:, None], axis=0))
    size_floor = jnp.maximum(group_sizes, 1.0)
    group_mean = reward_sums / size_floor
    variance = squares / size_floor - group_mean * group_mean
    group_scale = jnp.sqrt(jnp.maximum(variance, 1.0))
    advantage = (rewards - lax.optimization_barrier(jnp.sum(membership * group_mean[None, :], axis=1))) / lax.optimization_barrier(jnp.sum(membership * group_scale[None, :], axis=1))
    masked = action_mask.astype(jnp.float32)
    mask_total = jnp.maximum(jnp.sum(masked), 1.0)
    loss_weight = (-masked * advantage[:, None] / mask_total).reshape(-1)
    logit_grad = (loss_weight[:, None] * (picked - jnp.exp(log_all))).astype(jnp.bfloat16)
    grad_head = jnp.dot(jnp.transpose(head_input), logit_grad, preferred_element_type=jnp.float32).astype(jnp.bfloat16)
    pool_grad = lax.optimization_barrier(jnp.sum(jnp.dot(logit_grad, jnp.transpose(head_weight), preferred_element_type=jnp.float32).reshape(EPISODES, NACT, HID), axis=1))

    def accumulate(running, element):
        frame_rows, length, pull = element
        pre_act = jnp.dot(frame_rows, proj_weight, preferred_element_type=jnp.float32)
        token_mask = (positions < length).astype(jnp.float32) / length.astype(jnp.float32)
        act_grad = (token_mask[:, None] * pull[None, :] * gelu_slope(pre_act)).astype(jnp.bfloat16)
        return (running + jnp.dot(jnp.transpose(frame_rows), act_grad, preferred_element_type=jnp.float32), None)
    start_grad = jnp.zeros((VIS, HID), jnp.float32)
    grad_proj, _ = lax.scan(accumulate, start_grad, (frames, lengths, pool_grad))
    return (logprobs, grad_proj.astype(jnp.bfloat16), grad_head)
```

```python
import functools
import math

import jax
import jax.numpy as jnp
from jax import lax
from jax.experimental import pallas as pl
from jax.experimental.pallas import tpu as pltpu
from jax.sharding import Mesh
from jax.sharding import PartitionSpec as P


F32, BF16 = jnp.float32, jnp.bfloat16
HD = 128
HEADS_HERE = 4
COLS = 512
ATT = 2048
VIS = 2176
ROWS = 136
HID_HERE = 1024
SEQ = 1024
CHUNKS = 4
CH = SEQ // CHUNKS
NBINS = 256
SQRT_HALF = 0.7071067811865476
INV_ROOT_TAU = 0.3989422804014327
NEG_LARGE = -1e30
EXP2_SCALE = math.log2(math.e) / math.sqrt(HD)
VMEM_LIMIT = 56 * 1024 * 1024


def params(dims=1):
    return pltpu.CompilerParams(
        dimension_semantics=("arbitrary",) * dims, vmem_limit_bytes=VMEM_LIMIT
    )


def cost(flops, nbytes, trans=0):
    return pl.CostEstimate(flops=flops, bytes_accessed=nbytes, transcendentals=trans)


def shifted(x, axis, by):
    count = lax.axis_size(axis)
    return lax.ppermute(x, axis, [(i, (i + by) % count) for i in range(count)])


def dealt(x, axes):
    return lax.all_to_all(x, axes, 0, 0, tiled=True)


def pack_kernel(q_ref, k_ref, v_ref, o_ref):
    o_ref[0, 0] = q_ref[0]
    o_ref[0, 1] = k_ref[0]
    o_ref[0, 2] = v_ref[0]


def pack(q, k, v):
    spec = pl.BlockSpec((1, 128, COLS), lambda i: (i // 4, 0, i % 4))
    return pl.pallas_call(
        pack_kernel,
        out_shape=jax.ShapeDtypeStruct((8, 3, 128, COLS), BF16),
        grid=(8,),
        in_specs=[spec] * 3,
        out_specs=pl.BlockSpec((1, 3, 128, COLS), lambda i: (i, 0, 0, 0)),
        compiler_params=params(),
        cost_estimate=cost(0, 6 << 20),
        name="pack",
    )(q, k, v)


def attend_kernel(len_ref, q_ref, k_ref, v_ref, o_ref):
    q = q_ref[...].reshape(CH, HD)
    k = k_ref[...].reshape(SEQ, HD)
    v = v_ref[...].reshape(SEQ, HD)
    s = lax.dot_general(q, k, (((1,), (1,)), ((), ())), preferred_element_type=F32)
    at = lax.broadcasted_iota(jnp.int32, (CH, SEQ), 1)
    s = jnp.where(at < len_ref[0], s, NEG_LARGE)
    top = jnp.max(s, axis=-1, keepdims=True)
    p = jnp.exp2((s - top) * EXP2_SCALE)
    total = jnp.sum(p, axis=-1, keepdims=True)
    w = jnp.dot(p.astype(BF16), v, preferred_element_type=F32)
    o_ref[...] = (w / total).astype(BF16)


def attend(got, length, chunk):
    blocks = CH // 128

    def part(which, count):
        return pl.BlockSpec(
            (count, 1, 128, HD),
            lambda h, n: (chunk if which == 0 else 0, which, 0, h),
        )

    return pl.pallas_call(
        attend_kernel,
        out_shape=jax.ShapeDtypeStruct((CH, COLS), BF16),
        grid_spec=pltpu.PrefetchScalarGridSpec(
            num_scalar_prefetch=1,
            grid=(HEADS_HERE,),
            in_specs=[part(0, blocks), part(1, 8), part(2, 8)],
            out_specs=pl.BlockSpec((CH, HD), lambda h, n: (0, h)),
        ),
        compiler_params=params(),
        cost_estimate=cost(4 * CH * SEQ * COLS, 3 << 20, 4 * CH * SEQ),
        name="attend",
    )(length, got, got, got)


def frames_kernel(idx_ref, a_ref, b_ref, c_ref, d_ref, fm_ref, *rest):
    o_ref, piece, acc = rest[-3:]
    step = pl.program_id(0)
    for i, ref in enumerate((a_ref, b_ref, c_ref, d_ref)):

        @pl.when(step == i)
        def _():
            piece[...] = ref[...]

    term = jnp.dot(piece[...], fm_ref[...], preferred_element_type=F32)

    @pl.when(step == 0)
    def _():
        acc[...] = term

    @pl.when((step > 0) & (step < 3))
    def _():
        acc[...] += term

    @pl.when(step == 3)
    def _():
        o_ref[...] = (acc[...] + term).astype(BF16)


def frames_of(idx, pieces, frame_map, chunk, before):
    whole = pl.BlockSpec((CH, COLS), lambda k, n: (0, 0))
    more = [] if before is None else [before]
    return pl.pallas_call(
        frames_kernel,
        out_shape=jax.ShapeDtypeStruct((SEQ, VIS), BF16),
        grid_spec=pltpu.PrefetchScalarGridSpec(
            num_scalar_prefetch=1,
            grid=(4,),
            in_specs=[whole] * 4
            + [pl.BlockSpec((COLS, VIS), lambda k, n: (n[k], 0))]
            + [pl.BlockSpec(memory_space=pl.ANY)] * len(more),
            out_specs=pl.BlockSpec((CH, VIS), lambda k, n: (chunk, 0)),
            scratch_shapes=[pltpu.VMEM((CH, COLS), BF16), pltpu.VMEM((CH, VIS), F32)],
        ),
        input_output_aliases={} if before is None else {6: 0},
        compiler_params=params(),
        cost_estimate=cost(2 * CH * ATT * VIS, 11 << 20),
        name="frames",
    )(idx, *pieces, frame_map, *more)


def hidden_kernel(chunk, len_ref, f_ref, w_ref, *rest):
    slope_ref, pool_ref = rest[-2:]
    t = jnp.dot(f_ref[...], w_ref[...], preferred_element_type=F32)
    cdf = 0.5 * (1.0 + lax.erf(t * SQRT_HALF))
    at = lax.broadcasted_iota(jnp.int32, t.shape, 0) + chunk * CH
    live = at < len_ref[0]
    slope = cdf + t * jnp.exp(-0.5 * t * t) * INV_ROOT_TAU
    slope_ref[...] = jnp.where(live, slope, 0.0).astype(BF16)
    part = jnp.sum(jnp.where(live, t * cdf, 0.0), axis=0, keepdims=True)
    pool_ref[...] = jnp.broadcast_to(part, pool_ref.shape)


def hidden_of(length, frames, weight, chunk, before):
    tile = 256
    more = [] if before is None else [before]
    return pl.pallas_call(
        functools.partial(hidden_kernel, chunk),
        out_shape=(
            jax.ShapeDtypeStruct((SEQ, HID_HERE), BF16),
            jax.ShapeDtypeStruct((8, HID_HERE), F32),
        ),
        grid_spec=pltpu.PrefetchScalarGridSpec(
            num_scalar_prefetch=1,
            grid=(HID_HERE // tile,),
            in_specs=[
                pl.BlockSpec((CH, VIS), lambda j, n: (chunk, 0)),
                pl.BlockSpec((VIS, tile), lambda j, n: (0, j)),
            ]
            + [pl.BlockSpec(memory_space=pl.ANY)] * len(more),
            out_specs=(
                pl.BlockSpec((CH, tile), lambda j, n: (chunk, j)),
                pl.BlockSpec((8, tile), lambda j, n: (0, j)),
            ),
        ),
        input_output_aliases={} if before is None else {3: 0},
        compiler_params=params(),
        cost_estimate=cost(2 * CH * HID_HERE * VIS, 6 << 20, 2 * CH * HID_HERE),
        name="hidden",
    )(length, frames, weight, *more)


def grad_kernel(core_ref, f_ref, s_ref, keep_ref, send_ref, total):
    for r in range(VIS // 128):
        total[r * 128 : (r + 1) * 128, :] = lax.dot_general(
            f_ref[:, r * 128 : (r + 1) * 128],
            s_ref[...],
            (((0,), (0,)), ((), ())),
            preferred_element_type=F32,
        )
    core = core_ref[0]
    for b in range(8):
        mine = pl.multiple_of((2 * b + core) * ROWS, 8)
        other = pl.multiple_of((2 * b + 1 - core) * ROWS, 8)
        keep_ref[b, 0] = total[pl.ds(mine, ROWS), :].astype(BF16)
        send_ref[b, 0] = total[pl.ds(other, ROWS), :].astype(BF16)


def grad_of(core, frames, slope):
    out = jax.ShapeDtypeStruct((8, 2, ROWS, COLS), BF16)
    spec = pl.BlockSpec((8, 1, ROWS, COLS), lambda j, n: (0, j, 0, 0))
    return pl.pallas_call(
        grad_kernel,
        out_shape=(out, out),
        grid_spec=pltpu.PrefetchScalarGridSpec(
            num_scalar_prefetch=1,
            grid=(2,),
            in_specs=[
                pl.BlockSpec((SEQ, VIS), lambda j, n: (0, 0)),
                pl.BlockSpec((SEQ, COLS), lambda j, n: (0, j)),
            ],
            out_specs=(spec, spec),
            scratch_shapes=[pltpu.VMEM((VIS, COLS), F32)],
        ),
        compiler_params=params(),
        cost_estimate=cost(2 * SEQ * HID_HERE * VIS, 11 << 20),
        name="grad",
    )(core, frames, slope)


def logit_kernel(part_ref, act_ref, weight_ref, inv_ref, hw_ref, lp_ref, lg_ref, scale_ref):
    logits = (part_ref[0] + part_ref[1]) + (part_ref[2] + part_ref[3])
    top = jnp.max(logits, axis=-1, keepdims=True)
    down = logits - top
    log_all = down - jnp.log(jnp.sum(jnp.exp(down), axis=-1, keepdims=True))
    at = lax.broadcasted_iota(jnp.int32, logits.shape, 2)
    picked = (at == act_ref[...]).astype(F32)
    lp = jnp.sum(picked * log_all, axis=-1, keepdims=True)
    lp_ref[...] = jnp.broadcast_to(lp, lp_ref.shape)
    grad = (weight_ref[...] * (picked - jnp.exp(log_all))).astype(BF16)
    lg_ref[...] = grad
    for c in range(2):
        back = lax.dot_general(
            grad[c], hw_ref[...], (((1,), (1,)), ((), ())), preferred_element_type=F32
        )
        pool = jnp.sum(back, axis=0, keepdims=True) * inv_ref[c]
        scale_ref[c] = jnp.broadcast_to(pool, scale_ref.shape[1:])


def logit_parts(parts, acts, weights, inv, hw):
    return pl.pallas_call(
        logit_kernel,
        out_shape=(
            jax.ShapeDtypeStruct((2, 8, 128), F32),
            jax.ShapeDtypeStruct((2, 8, NBINS), BF16),
            jax.ShapeDtypeStruct((2, 8, HID_HERE), F32),
        ),
        in_specs=[pl.BlockSpec(memory_space=pltpu.VMEM)] * 3
        + [pl.BlockSpec(memory_space=pltpu.SMEM), pl.BlockSpec(memory_space=pltpu.VMEM)],
        compiler_params=pltpu.CompilerParams(vmem_limit_bytes=VMEM_LIMIT),
        cost_estimate=cost(8 << 20, 1 << 20, 8192),
        name="logit",
    )(parts, acts, weights, inv, hw)


def scale_kernel(core_ref, keep_ref, got_ref, scale_ref, head_ref, lg_ref, o_ref):
    core = core_ref[0]
    mine = scale_ref[core][0:1]
    other = scale_ref[1 - core][0:1]
    lower = jnp.concatenate([lg_ref[core].astype(F32), jnp.zeros((8, NBINS), F32)], axis=1)
    for x in range(2):
        cols = slice(x * COLS, (x + 1) * COLS)
        top = (
            keep_ref[0, x].astype(F32) * mine[:, cols] + got_ref[0, x].astype(F32) * other[:, cols]
        )
        o_ref[0, x] = jnp.concatenate([top, head_ref[:, cols].astype(F32), lower], axis=0).astype(
            BF16
        )


def scaled(core, keep, got, scale, head_input, lgrad):
    spec = pl.BlockSpec((1, 2, ROWS, COLS), lambda i, n: (i, 0, 0, 0))
    return pl.pallas_call(
        scale_kernel,
        out_shape=jax.ShapeDtypeStruct((8, 2, ROWS + 16, COLS), BF16),
        grid_spec=pltpu.PrefetchScalarGridSpec(
            num_scalar_prefetch=1,
            grid=(8,),
            in_specs=[
                spec,
                spec,
                pl.BlockSpec((2, 8, HID_HERE), lambda i, n: (0, 0, 0)),
                pl.BlockSpec((8, HID_HERE), lambda i, n: (0, 0)),
                pl.BlockSpec((2, 8, NBINS), lambda i, n: (0, 0, 0)),
            ],
            out_specs=pl.BlockSpec((1, 2, ROWS + 16, COLS), lambda i, n: (i, 0, 0, 0)),
        ),
        compiler_params=params(),
        cost_estimate=cost(8 << 20, 7 << 20),
        name="scaled",
    )(core, keep, got, scale, head_input, lgrad)


def episode_facts(lengths, actions, action_mask, group_ids, rewards):
    columns = [
        rewards[:, None],
        group_ids[:, None].astype(F32),
        lengths[:, None].astype(F32),
        jnp.zeros((2, 5), F32),
        actions.astype(F32),
        jnp.zeros((2, 1), F32),
        action_mask.astype(F32),
        jnp.zeros((2, 105), F32),
    ]
    return jnp.concatenate(columns, axis=1)


def loss_terms(facts, here):
    every = facts.reshape(32, 128)
    gains, groups, masks = every[:, 0], every[:, 1], every[:, 16:23]
    member = (groups[:, None] == jnp.arange(4, dtype=F32)[None, :]).astype(F32)
    sums = jnp.sum(member * gains[:, None], axis=0)
    squares = jnp.sum(member * (gains * gains)[:, None], axis=0)
    sizes = jnp.maximum(jnp.sum(member, axis=0), 1.0)
    mean = sums / sizes
    spread = jnp.sqrt(jnp.maximum(squares / sizes - mean * mean, 1.0))
    count = jnp.maximum(jnp.sum(masks), 1.0)
    own = (here[:, 1:2] == jnp.arange(4, dtype=F32)[None, :]).astype(F32)
    advantage = (here[:, 0] - jnp.sum(own * mean[None, :], axis=1)) / jnp.sum(
        own * spread[None, :], axis=1
    )
    return -here[:, 16:24] * advantage[:, None] / count, here[:, 8:16], 1.0 / here[:, 2]


def per_device(
    queries,
    keys,
    values,
    lengths,
    frame_map,
    proj_weight,
    head_weight,
    act_embed,
    actions,
    action_mask,
    group_ids,
    rewards,
):
    xh = lax.axis_index("xh")
    y = lax.axis_index("y")
    z = lax.axis_index("z")
    xl = lax.axis_index("xl")
    core = lax.axis_index("c")
    core1 = core.reshape(1)
    length = lax.dynamic_slice_in_dim(lengths, xh, 1)

    got = dealt(pack(queries, keys, values), ("xh", "y"))

    first = xh == 0
    hw_other, ae_other = shifted(head_weight, "xh", 1), shifted(act_embed, "xh", 1)

    def both(mine, other, axis):
        return jnp.concatenate(
            [jnp.where(first, mine, other), jnp.where(first, other, mine)], axis=axis
        )

    hw = both(head_weight, hw_other, 0)
    embed = jnp.pad(both(act_embed, ae_other, 1), ((0, 1), (0, 0)))

    shard, facts, _ = lax.optimization_barrier(
        (
            proj_weight,
            episode_facts(lengths, actions, action_mask, group_ids, rewards),
            got,
        )
    )
    own_rows = dealt(jnp.broadcast_to(shard[None], (16, ROWS, COLS)), ("z", "xl", "xh"))
    other_rows = shifted(own_rows, "c", 1)
    lead = core == 0
    rows = jnp.stack(
        [jnp.where(lead, own_rows, other_rows), jnp.where(lead, other_rows, own_rows)]
    )
    weight = (
        rows.reshape(2, 8, 2, ROWS, COLS).transpose(1, 0, 3, 2, 4).reshape(VIS, HID_HERE)
    )
    facts = dealt(jnp.broadcast_to(facts[None], (16, 2, 128)), ("z", "xl", "c"))
    pair = lax.dynamic_slice(
        facts.reshape(8, 2, 2, 128), (z * 2 + xl, 0, xh, 0), (1, 2, 1, 128)
    ).reshape(2, 128)
    loss_weight, acts, inverse = loss_terms(facts, pair)
    wide_weight = jnp.broadcast_to(loss_weight[:, :, None], (2, 8, NBINS))
    wide_acts = jnp.broadcast_to(acts[:, :, None], (2, 8, NBINS)).astype(jnp.int32)

    idx = (y + jnp.array([0, 3, 1, 2], jnp.int32)) % 4
    frames, slope, pools = None, None, []
    for chunk in range(CHUNKS):
        a = attend(got, length, chunk)
        b = shifted(a, "y", 1)
        c = shifted(a, "y", -1)
        d = shifted(b, "y", 1) if chunk % 2 == 0 else shifted(c, "y", -1)
        frames = frames_of(idx, (a, b, c, d), frame_map, chunk, frames)
        slope, pool = hidden_of(length, frames, weight, chunk, slope)
        pools.append(pool)
    pooled = ((pools[0] + pools[1]) + (pools[2] + pools[3])) / length.astype(F32)
    head_input = (pooled + embed).astype(BF16)
    part = jnp.dot(head_input, hw, preferred_element_type=F32)
    parts = dealt(jnp.broadcast_to(part[None], (8, 8, NBINS)), ("y", "c"))

    keep, send = grad_of(core1, frames, slope)
    arrived = shifted(send, "c", 1)

    logprob, lgrad, scale = logit_parts(
        parts.reshape(4, 2, 8, NBINS), wide_acts, wide_weight, inverse, hw
    )
    summed = scaled(core1, keep, arrived, scale, head_input, lgrad)
    dealt_out = dealt(summed.reshape(16, ROWS + 16, COLS), ("z", "xl", "xh"))
    grad_proj = jnp.sum(dealt_out[:, :ROWS].astype(F32), axis=0).astype(BF16)

    own_head = dealt_out[:, ROWS:]
    other_head = shifted(own_head, "c", 1)
    heads = jnp.stack([own_head, other_head])
    lefts = heads[:, :, :8].reshape(256, COLS)
    rights = heads[:, :, 8:, :NBINS].reshape(256, NBINS)
    grad_head = lax.dot_general(
        lefts, rights, (((0,), (0,)), ((), ())), preferred_element_type=F32
    ).astype(BF16)

    lp_mine = lax.dynamic_index_in_dim(logprob[:, :7, 0], core, 0)
    lp_other = shifted(lp_mine, "xh", 1)
    logprobs = both(lp_mine, lp_other, 0)
    return logprobs, grad_proj, grad_head


def solution(mesh):
    fine = Mesh(mesh.devices.reshape(2, 4, 4, 2, 2), ("xh", "y", "z", "xl", "c"))
    cp, grp = ("xh", "y"), ("z", "xl", "c")
    in_specs = (
        P(grp, cp, None),
        P(grp, cp, None),
        P(grp, cp, None),
        P(grp),
        P(),
        P(grp, cp),
        P(cp, None),
        P(None, cp),
        P(grp, None),
        P(grp, None),
        P(grp),
        P(grp),
    )
    out_specs = (P(grp, None), P(grp, cp), P(cp, None))
    return jax.shard_map(
        per_device, mesh=fine, in_specs=in_specs, out_specs=out_specs, check_vma=False
    )
```

```python
import functools
import math

import jax
import jax.numpy as jnp
from jax import lax
from jax.experimental import pallas as pl
from jax.experimental.pallas import tpu as pltpu
from jax.sharding import Mesh
from jax.sharding import PartitionSpec as P


F32, BF16 = jnp.float32, jnp.bfloat16
HD = 128
HEADS_HERE = 4
COLS = 512
ATT = 2048
VIS = 2176
ROWS = 136
HID_HERE = 1024
SEQ = 1024
CHUNKS = 2
CH = SEQ // CHUNKS
NBINS = 256
SQRT_HALF = 0.7071067811865476
INV_ROOT_TAU = 0.3989422804014327
NEG_LARGE = -1e30
EXP2_SCALE = math.log2(math.e) / math.sqrt(HD)
VMEM_LIMIT = 67043328


def params(dims=1):
    return pltpu.CompilerParams(
        dimension_semantics=("arbitrary",) * dims, vmem_limit_bytes=VMEM_LIMIT
    )


def cost(flops, nbytes, trans=0):
    return pl.CostEstimate(flops=flops, bytes_accessed=nbytes, transcendentals=trans)


def shifted(x, axis, by):
    count = lax.axis_size(axis)
    return lax.ppermute(x, axis, [(i, (i + by) % count) for i in range(count)])


def dealt(x, axes):
    return lax.all_to_all(x, axes, 0, 0, tiled=True)


def pack_kernel(q_ref, k_ref, v_ref, o_ref):
    for i, ref in enumerate((q_ref, k_ref, v_ref)):
        for j in range(2):
            o_ref[j, i] = ref[0, :, j * COLS : (j + 1) * COLS]


def pack(q, k, v):
    spec = pl.BlockSpec((1, 128, 2 * COLS), lambda i: (i // 2, 0, i % 2))
    return pl.pallas_call(
        pack_kernel,
        out_shape=jax.ShapeDtypeStruct((8, 3, 128, COLS), BF16),
        grid=(4,),
        in_specs=[spec] * 3,
        out_specs=pl.BlockSpec((2, 3, 128, COLS), lambda i: (i, 0, 0, 0)),
        compiler_params=params(),
        cost_estimate=cost(0, 6 << 20),
        name="pack",
    )(q, k, v)


def attend_kernel(len_ref, q_ref, k_ref, v_ref, *rest):
    o_ref = rest[-1]
    k = k_ref[...].reshape(SEQ, HD)
    v = v_ref[...].reshape(SEQ, HD)
    at = lax.broadcasted_iota(jnp.int32, (1, SEQ), 1)
    bias = jnp.where(at < len_ref[0], 0.0, NEG_LARGE)
    for r in range(CH // 256):
        q = q_ref[2 * r : 2 * r + 2].reshape(256, HD)
        s = lax.dot_general(q, k, (((1,), (1,)), ((), ())), preferred_element_type=F32)
        s = s + bias
        top = jnp.max(s, axis=-1, keepdims=True)
        p = jnp.exp2((s - top) * EXP2_SCALE)
        total = jnp.sum(p, axis=-1, keepdims=True)
        w = jnp.dot(p.astype(BF16), v, preferred_element_type=F32)
        o_ref[r * 256 : (r + 1) * 256, :] = (w / total).astype(BF16)


def attend(got, length, chunk, after):
    blocks = CH // 128

    def part(which, count):
        return pl.BlockSpec(
            (count, 1, 128, HD),
            lambda h, n: (chunk if which == 0 else 0, which, 0, h),
        )

    return pl.pallas_call(
        attend_kernel,
        out_shape=jax.ShapeDtypeStruct((CH, COLS), BF16),
        grid_spec=pltpu.PrefetchScalarGridSpec(
            num_scalar_prefetch=1,
            grid=(HEADS_HERE,),
            in_specs=[part(0, blocks), part(1, 8), part(2, 8)]
            + [pl.BlockSpec(memory_space=pl.ANY)] * len(after),
            out_specs=pl.BlockSpec((CH, HD), lambda h, n: (0, h)),
        ),
        compiler_params=params(),
        cost_estimate=cost(4 * CH * SEQ * COLS, 3 << 20, 4 * CH * SEQ),
        name="attend",
    )(length, got, got, got, *after)


def frames_kernel(idx_ref, a_ref, b_ref, c_ref, d_ref, fm_ref, last_ref, *rest):
    o_ref, full = rest[-2:]
    step = pl.program_id(0)

    @pl.when(step == 0)
    def _():
        for i, ref in enumerate((a_ref, b_ref, c_ref, d_ref)):
            full[:, pl.ds(pl.multiple_of(idx_ref[i] * COLS, COLS), COLS)] = ref[...]

    term = jnp.dot(full[...], fm_ref[...], preferred_element_type=F32)
    o_ref[:, pl.ds(pl.multiple_of(step * 512, 512), 512)] = term.astype(BF16)

    @pl.when(step == 3)
    def _():
        term = jnp.dot(full[...], last_ref[...], preferred_element_type=F32)
        o_ref[:, 2048:] = term.astype(BF16)


def frames_of(idx, pieces, frame_map, chunk, before, after=()):
    whole = pl.BlockSpec((CH, COLS), lambda k, n: (0, 0))
    more = [] if before is None else [before]
    return pl.pallas_call(
        frames_kernel,
        out_shape=jax.ShapeDtypeStruct((SEQ, VIS), BF16),
        grid_spec=pltpu.PrefetchScalarGridSpec(
            num_scalar_prefetch=1,
            grid=(4,),
            in_specs=[whole] * 4
            + [
                pl.BlockSpec((ATT, 512), lambda k, n: (0, k)),
                pl.BlockSpec((ATT, 128), lambda k, n: (0, 16)),
            ]
            + [pl.BlockSpec(memory_space=pl.ANY)] * (len(more) + len(after)),
            out_specs=pl.BlockSpec((CH, VIS), lambda k, n: (chunk, 0)),
            scratch_shapes=[pltpu.VMEM((CH, ATT), BF16)],
        ),
        input_output_aliases={} if before is None else {7: 0},
        compiler_params=params(),
        cost_estimate=cost(2 * CH * ATT * VIS, 13 << 20),
        name="frames",
    )(idx, *pieces, frame_map, frame_map, *more, *after)


def assemble_kernel(z_ref, x_ref, core_ref, *refs):
    o_ref = refs[-1]
    lead = core_ref[0] == 0
    for k in range(4):
        for i in range(4):
            mine, other = refs[k][i].astype(F32), refs[4 + k][i].astype(F32)
            pair = [jnp.where(lead, mine, other), jnp.where(lead, other, mine)]
            x = x_ref[i]
            row = pl.multiple_of((z_ref[k] * 2 + x % 2) * 2 * ROWS, 2 * ROWS)
            col = pl.multiple_of((x // 2) * COLS, COLS)
            o_ref[pl.ds(row, 2 * ROWS), pl.ds(col, COLS)] = jnp.concatenate(pair, axis=0).astype(
                BF16
            )


def assemble(z_order, x_order, core, own, other):
    return pl.pallas_call(
        assemble_kernel,
        out_shape=jax.ShapeDtypeStruct((VIS, HID_HERE), BF16),
        in_specs=[pl.BlockSpec(memory_space=pltpu.SMEM)] * 3
        + [pl.BlockSpec(memory_space=pltpu.VMEM)] * 8,
        compiler_params=pltpu.CompilerParams(vmem_limit_bytes=VMEM_LIMIT),
        cost_estimate=cost(1 << 20, 9 << 20),
        name="assemble",
    )(z_order, x_order, core, *own, *other)


def hidden_kernel(chunk, len_ref, f_ref, w_ref, *rest):
    slope_ref, pool_ref = rest[-2:]
    t = jnp.dot(f_ref[...], w_ref[...], preferred_element_type=F32)
    cdf = 0.5 * (1.0 + lax.erf(t * SQRT_HALF))
    at = lax.broadcasted_iota(jnp.int32, t.shape, 0) + chunk * CH
    live = at < len_ref[0]
    slope = cdf + t * jnp.exp(-0.5 * t * t) * INV_ROOT_TAU
    slope_ref[...] = jnp.where(live, slope, 0.0).astype(BF16)
    part = jnp.sum(jnp.where(live, t * cdf, 0.0), axis=0, keepdims=True)
    pool_ref[...] = jnp.broadcast_to(part, pool_ref.shape)


def hidden_of(length, frames, weight, chunk, before):
    tile = 256
    more = [] if before is None else [before]
    return pl.pallas_call(
        functools.partial(hidden_kernel, chunk),
        out_shape=(
            jax.ShapeDtypeStruct((SEQ, HID_HERE), BF16),
            jax.ShapeDtypeStruct((8, HID_HERE), F32),
        ),
        grid_spec=pltpu.PrefetchScalarGridSpec(
            num_scalar_prefetch=1,
            grid=(HID_HERE // tile,),
            in_specs=[
                pl.BlockSpec((CH, VIS), lambda j, n: (chunk, 0)),
                pl.BlockSpec((VIS, tile), lambda j, n: (0, j)),
            ]
            + [pl.BlockSpec(memory_space=pl.ANY)] * len(more),
            out_specs=(
                pl.BlockSpec((CH, tile), lambda j, n: (chunk, j)),
                pl.BlockSpec((8, tile), lambda j, n: (0, j)),
            ),
        ),
        input_output_aliases={} if before is None else {3: 0},
        compiler_params=params(),
        cost_estimate=cost(2 * CH * HID_HERE * VIS, 6 << 20, 2 * CH * HID_HERE),
        name="hidden",
    )(length, frames, weight, *more)


def grad_kernel(core_ref, f_ref, s_ref, keep_ref, send_ref, total):
    for r in range(VIS // 128):
        total[r * 128 : (r + 1) * 128, :] = lax.dot_general(
            f_ref[:, r * 128 : (r + 1) * 128],
            s_ref[...],
            (((0,), (0,)), ((), ())),
            preferred_element_type=F32,
        )
    core = core_ref[0]
    for b in range(8):
        mine = pl.multiple_of((2 * b + core) * ROWS, 8)
        other = pl.multiple_of((2 * b + 1 - core) * ROWS, 8)
        keep_ref[b, 0] = total[pl.ds(mine, ROWS), :].astype(BF16)
        send_ref[b, 0] = total[pl.ds(other, ROWS), :].astype(BF16)


def grad_of(core, frames, slope):
    out = jax.ShapeDtypeStruct((8, 2, ROWS, COLS), BF16)
    spec = pl.BlockSpec((8, 1, ROWS, COLS), lambda j, n: (0, j, 0, 0))
    return pl.pallas_call(
        grad_kernel,
        out_shape=(out, out),
        grid_spec=pltpu.PrefetchScalarGridSpec(
            num_scalar_prefetch=1,
            grid=(2,),
            in_specs=[
                pl.BlockSpec((SEQ, VIS), lambda j, n: (0, 0)),
                pl.BlockSpec((SEQ, COLS), lambda j, n: (0, j)),
            ],
            out_specs=(spec, spec),
            scratch_shapes=[pltpu.VMEM((VIS, COLS), F32)],
        ),
        compiler_params=params(),
        cost_estimate=cost(2 * SEQ * HID_HERE * VIS, 11 << 20),
        name="grad",
    )(core, frames, slope)


def logit_kernel(part_ref, act_ref, weight_ref, inv_ref, hw_ref, lp_ref, lg_ref, scale_ref):
    logits = (part_ref[0] + part_ref[1]) + (part_ref[2] + part_ref[3])
    top = jnp.max(logits, axis=-1, keepdims=True)
    down = logits - top
    log_all = down - jnp.log(jnp.sum(jnp.exp(down), axis=-1, keepdims=True))
    at = lax.broadcasted_iota(jnp.int32, logits.shape, 2)
    picked = (at == act_ref[...]).astype(F32)
    lp = jnp.sum(picked * log_all, axis=-1, keepdims=True)
    lp_ref[...] = jnp.broadcast_to(lp, lp_ref.shape)
    grad = (weight_ref[...] * (picked - jnp.exp(log_all))).astype(BF16)
    lg_ref[...] = grad
    for c in range(2):
        back = lax.dot_general(
            grad[c], hw_ref[...], (((1,), (1,)), ((), ())), preferred_element_type=F32
        )
        pool = jnp.sum(back, axis=0, keepdims=True) * inv_ref[c]
        scale_ref[c] = jnp.broadcast_to(pool, scale_ref.shape[1:])


def logit_parts(parts, acts, weights, inv, hw):
    return pl.pallas_call(
        logit_kernel,
        out_shape=(
            jax.ShapeDtypeStruct((2, 8, 128), F32),
            jax.ShapeDtypeStruct((2, 8, NBINS), BF16),
            jax.ShapeDtypeStruct((2, 8, HID_HERE), F32),
        ),
        in_specs=[pl.BlockSpec(memory_space=pltpu.VMEM)] * 3
        + [pl.BlockSpec(memory_space=pltpu.SMEM), pl.BlockSpec(memory_space=pltpu.VMEM)],
        compiler_params=pltpu.CompilerParams(vmem_limit_bytes=VMEM_LIMIT),
        cost_estimate=cost(8 << 20, 1 << 20, 8192),
        name="logit",
    )(parts, acts, weights, inv, hw)


def scale_kernel(core_ref, keep_ref, got_ref, scale_ref, head_ref, lg_ref, o_ref):
    core = core_ref[0]
    mine = scale_ref[core][0:1]
    other = scale_ref[1 - core][0:1]
    lower = jnp.concatenate([lg_ref[core].astype(F32), jnp.zeros((8, NBINS), F32)], axis=1)
    for b in range(2):
        for x in range(2):
            cols = slice(x * COLS, (x + 1) * COLS)
            top = (
                keep_ref[b, x].astype(F32) * mine[:, cols]
                + got_ref[b, x].astype(F32) * other[:, cols]
            )
            o_ref[b, x] = jnp.concatenate(
                [top, head_ref[:, cols].astype(F32), lower], axis=0
            ).astype(BF16)


def scaled(core, keep, got, scale, head_input, lgrad):
    spec = pl.BlockSpec((2, 2, ROWS, COLS), lambda i, n: (i, 0, 0, 0))
    return pl.pallas_call(
        scale_kernel,
        out_shape=jax.ShapeDtypeStruct((8, 2, ROWS + 16, COLS), BF16),
        grid_spec=pltpu.PrefetchScalarGridSpec(
            num_scalar_prefetch=1,
            grid=(4,),
            in_specs=[
                spec,
                spec,
                pl.BlockSpec((2, 8, HID_HERE), lambda i, n: (0, 0, 0)),
                pl.BlockSpec((8, HID_HERE), lambda i, n: (0, 0)),
                pl.BlockSpec((2, 8, NBINS), lambda i, n: (0, 0, 0)),
            ],
            out_specs=pl.BlockSpec((2, 2, ROWS + 16, COLS), lambda i, n: (i, 0, 0, 0)),
        ),
        compiler_params=params(),
        cost_estimate=cost(8 << 20, 7 << 20),
        name="scaled",
    )(core, keep, got, scale, head_input, lgrad)


def episode_facts(lengths, actions, action_mask, group_ids, rewards):
    three = jnp.stack([rewards, group_ids.astype(F32), lengths.astype(F32)], axis=1)
    return jnp.concatenate(
        [
            jnp.pad(three, ((0, 0), (0, 5))),
            jnp.pad(actions.astype(F32), ((0, 0), (0, 1))),
            jnp.pad(action_mask.astype(F32), ((0, 0), (0, 1))),
        ],
        axis=1,
    )


def loss_terms(every, here):
    gains, groups, masks = every[:, 0], every[:, 1], every[:, 16:24]
    member = (groups[:, None] == jnp.arange(4, dtype=F32)[None, :]).astype(F32)
    sums = jnp.sum(member * gains[:, None], axis=0)
    squares = jnp.sum(member * (gains * gains)[:, None], axis=0)
    sizes = jnp.maximum(jnp.sum(member, axis=0), 1.0)
    mean = sums / sizes
    spread = jnp.sqrt(jnp.maximum(squares / sizes - mean * mean, 1.0))
    count = jnp.maximum(jnp.sum(masks), 1.0)
    own = (here[:, 1:2] == jnp.arange(4, dtype=F32)[None, :]).astype(F32)
    advantage = (here[:, 0] - jnp.sum(own * mean[None, :], axis=1)) / jnp.sum(
        own * spread[None, :], axis=1
    )
    return -here[:, 16:24] * advantage[:, None] / count, here[:, 8:16], 1.0 / here[:, 2]


def per_device(
    queries,
    keys,
    values,
    lengths,
    frame_map,
    proj_weight,
    head_weight,
    act_embed,
    actions,
    action_mask,
    group_ids,
    rewards,
):
    xh = lax.axis_index("xh")
    y = lax.axis_index("y")
    z = lax.axis_index("z")
    xl = lax.axis_index("xl")
    core = lax.axis_index("c")
    core1 = core.reshape(1)
    length = lax.dynamic_slice_in_dim(lengths, xh, 1)

    got = dealt(pack(queries, keys, values), ("xh", "y"))

    x = xh * 2 + xl
    line = ("xh", "xl")
    row = [proj_weight] + [shifted(proj_weight, line, by) for by in (1, -1, 2)]
    x_order = (x + jnp.array([0, 3, 1, 2], jnp.int32)) % 4
    block = jnp.stack(row)
    up, down = shifted(block, "z", 1), shifted(block, "z", -1)
    half = jnp.concatenate([shifted(up[:2], "z", 1), shifted(down[2:], "z", -1)])
    z_order = (z + jnp.array([0, 3, 1, 2], jnp.int32)) % 4
    own = (block, up, down, half)
    other = [shifted(w, "c", 1) for w in own]
    weight = assemble(z_order, x_order, core1, own, other)

    first = xh == 0
    hw_other, ae_other = shifted(head_weight, "xh", 1), shifted(act_embed, "xh", 1)

    def both(mine, other, axis):
        return jnp.concatenate(
            [jnp.where(first, mine, other), jnp.where(first, other, mine)], axis=axis
        )

    hw = both(head_weight, hw_other, 0)
    embed = jnp.pad(both(act_embed, ae_other, 1), ((0, 1), (0, 0)))

    facts = episode_facts(lengths, actions, action_mask, group_ids, rewards)
    facts = jnp.concatenate([facts, shifted(facts, "c", 1)])
    pair = lax.dynamic_slice(facts.reshape(2, 2, 24), (0, xh, 0), (2, 1, 24)).reshape(2, 24)
    pair = jnp.where(core == 0, pair, pair[::-1])
    facts = jnp.concatenate([facts, shifted(facts, "xl", 1)])
    facts = jnp.concatenate([facts] + [shifted(facts, "z", by) for by in (1, 2, 3)])
    loss_weight, acts, inverse = loss_terms(facts, pair)
    wide_weight = jnp.broadcast_to(loss_weight[:, :, None], (2, 8, NBINS))
    wide_acts = jnp.broadcast_to(acts[:, :, None], (2, 8, NBINS)).astype(jnp.int32)

    idx = (y + jnp.array([0, 3, 1, 2], jnp.int32)) % 4
    a0 = attend(got, length, 0, (wide_weight, wide_acts, hw, embed, up, down))
    a1 = attend(got, length, 1, ())
    b0 = shifted(a0, "y", 1)
    c0 = shifted(a0, "y", -1)
    b1 = shifted(a1, "y", 1)
    c1 = shifted(a1, "y", -1)
    d0 = shifted(b0, "y", 1)
    d1 = shifted(c1, "y", -1)

    frames = frames_of(idx, (a0, b0, c0, d0), frame_map, 0, None, (weight,))
    slope, pool0 = hidden_of(length, frames, weight, 0, None)
    frames = frames_of(idx, (a1, b1, c1, d1), frame_map, 1, frames)
    slope, pool1 = hidden_of(length, frames, weight, 1, slope)
    pooled = (pool0 + pool1) / length.astype(F32)
    head_input = (pooled + embed).astype(BF16)
    part = jnp.dot(head_input, hw, preferred_element_type=F32)
    parts = dealt(jnp.broadcast_to(part[None], (8, 8, NBINS)), ("y", "c"))
    keep, send = grad_of(core1, frames, slope)
    arrived = shifted(send, "c", 1)

    logprob, lgrad, scale = logit_parts(
        parts.reshape(4, 2, 8, NBINS), wide_acts, wide_weight, inverse, hw
    )
    summed = scaled(core1, keep, arrived, scale, head_input, lgrad)
    dealt_out = dealt(summed.reshape(16, ROWS + 16, COLS), ("z", "xl", "xh"))
    grad_proj = jnp.sum(dealt_out[:, :ROWS].astype(F32), axis=0).astype(BF16)

    own_head = dealt_out[:, ROWS:]
    other_head = shifted(own_head, "c", 1)
    heads = jnp.stack([own_head, other_head])
    lefts = heads[:, :, :8].reshape(256, COLS)
    rights = heads[:, :, 8:, :NBINS].reshape(256, NBINS)
    grad_head = lax.dot_general(
        lefts, rights, (((0,), (0,)), ((), ())), preferred_element_type=F32
    ).astype(BF16)

    lp_mine = lax.dynamic_index_in_dim(logprob[:, :7, 0], core, 0)
    lp_other = shifted(lp_mine, "xh", 1)
    logprobs = both(lp_mine, lp_other, 0)
    return logprobs, grad_proj, grad_head


def solution(mesh):
    fine = Mesh(mesh.devices.reshape(2, 4, 4, 2, 2), ("xh", "y", "z", "xl", "c"))
    cp, grp = ("xh", "y"), ("z", "xl", "c")
    in_specs = (
        P(grp, cp, None),
        P(grp, cp, None),
        P(grp, cp, None),
        P(grp),
        P(),
        P(grp, cp),
        P(cp, None),
        P(None, cp),
        P(grp, None),
        P(grp, None),
        P(grp),
        P(grp),
    )
    out_specs = (P(grp, None), P(grp, cp), P(cp, None))
    return jax.shard_map(
        per_device, mesh=fine, in_specs=in_specs, out_specs=out_specs, check_vma=False
    )
```

```python
import functools
import math

import jax
import jax.numpy as jnp
from jax import lax
from jax.experimental import pallas as pl
from jax.experimental.pallas import tpu as pltpu
from jax.sharding import Mesh
from jax.sharding import PartitionSpec as P


F32, BF16 = jnp.float32, jnp.bfloat16
HD = 128
HEADS_HERE = 4
COLS = 512
ATT = 2048
VIS = 2176
ROWS = 136
HID_HERE = 1024
SEQ = 1024
CHUNKS = 2
CH = SEQ // CHUNKS
NBINS = 256
SQRT_HALF = 0.7071067811865476
INV_ROOT_TAU = 0.3989422804014327
NEG_LARGE = -1e30
EXP2_SCALE = math.log2(math.e) / math.sqrt(HD)
VMEM_LIMIT = 67043328


def params(dims=1):
    return pltpu.CompilerParams(
        dimension_semantics=("arbitrary",) * dims, vmem_limit_bytes=VMEM_LIMIT
    )


def cost(flops, nbytes, trans=0):
    return pl.CostEstimate(flops=flops, bytes_accessed=nbytes, transcendentals=trans)


def shifted(x, axis, by):
    count = lax.axis_size(axis)
    return lax.ppermute(x, axis, [(i, (i + by) % count) for i in range(count)])


def dealt(x, axes):
    return lax.all_to_all(x, axes, 0, 0, tiled=True)


def pack_kernel(q_ref, k_ref, v_ref, o_ref):
    for i, ref in enumerate((q_ref, k_ref, v_ref)):
        for j in range(2):
            o_ref[j, i] = ref[0, :, j * COLS : (j + 1) * COLS]


def pack(q, k, v):
    spec = pl.BlockSpec((1, 128, 2 * COLS), lambda i: (i // 2, 0, i % 2))
    return pl.pallas_call(
        pack_kernel,
        out_shape=jax.ShapeDtypeStruct((8, 3, 128, COLS), BF16),
        grid=(4,),
        in_specs=[spec] * 3,
        out_specs=pl.BlockSpec((2, 3, 128, COLS), lambda i: (i, 0, 0, 0)),
        compiler_params=params(),
        cost_estimate=cost(0, 6 << 20),
        name="pack",
    )(q, k, v)


def attend_kernel(len_ref, q_ref, k_ref, v_ref, *rest):
    o_ref = rest[-1]
    k = k_ref[...].reshape(SEQ, HD)
    v = v_ref[...].reshape(SEQ, HD)
    at = lax.broadcasted_iota(jnp.int32, (1, SEQ), 1)
    bias = jnp.where(at < len_ref[0], 0.0, NEG_LARGE)
    for r in range(CH // 256):
        q = q_ref[2 * r : 2 * r + 2].reshape(256, HD)
        s = lax.dot_general(q, k, (((1,), (1,)), ((), ())), preferred_element_type=F32)
        s = s + bias
        top = jnp.max(s, axis=-1, keepdims=True)
        p = jnp.exp2((s - top) * EXP2_SCALE)
        total = jnp.sum(p, axis=-1, keepdims=True)
        w = jnp.dot(p.astype(BF16), v, preferred_element_type=F32)
        o_ref[r * 256 : (r + 1) * 256, :] = (w / total).astype(BF16)


def attend(got, length, chunk, after):
    blocks = CH // 128

    def part(which, count):
        return pl.BlockSpec(
            (count, 1, 128, HD),
            lambda h, n: (chunk if which == 0 else 0, which, 0, h),
        )

    return pl.pallas_call(
        attend_kernel,
        out_shape=jax.ShapeDtypeStruct((CH, COLS), BF16),
        grid_spec=pltpu.PrefetchScalarGridSpec(
            num_scalar_prefetch=1,
            grid=(HEADS_HERE,),
            in_specs=[part(0, blocks), part(1, 8), part(2, 8)]
            + [pl.BlockSpec(memory_space=pl.ANY)] * len(after),
            out_specs=pl.BlockSpec((CH, HD), lambda h, n: (0, h)),
        ),
        compiler_params=params(),
        cost_estimate=cost(4 * CH * SEQ * COLS, 3 << 20, 4 * CH * SEQ),
        name="attend",
    )(length, got, got, got, *after)


def chunk_kernel(chunk, idx_ref, len_ref, a_ref, b_ref, c_ref, d_ref, fm_ref, last_ref, w_ref, *rest):
    o_ref, slope_ref, pool_ref, full = rest[-4:]
    step = pl.program_id(0)

    @pl.when(step == 0)
    def _():
        for i, ref in enumerate((a_ref, b_ref, c_ref, d_ref)):
            full[:, pl.ds(pl.multiple_of(idx_ref[i] * COLS, COLS), COLS)] = ref[...]

    @pl.when(step < 4)
    def _():
        term = jnp.dot(full[...], fm_ref[...], preferred_element_type=F32)
        o_ref[:, pl.ds(pl.multiple_of(step * 512, 512), 512)] = term.astype(BF16)

    @pl.when(step == 3)
    def _():
        term = jnp.dot(full[...], last_ref[...], preferred_element_type=F32)
        o_ref[:, 2048:] = term.astype(BF16)

    @pl.when(step >= 4)
    def _():
        total = jnp.zeros((1, slope_ref.shape[1]), F32)
        for r in range(CH // 256):
            rows = slice(r * 256, (r + 1) * 256)
            t = jnp.dot(o_ref[rows, :], w_ref[...], preferred_element_type=F32)
            cdf = 0.5 * (1.0 + lax.erf(t * SQRT_HALF))
            at = lax.broadcasted_iota(jnp.int32, (256, 1), 0) + (chunk * CH + r * 256)
            live = (at < len_ref[0]).astype(F32)
            slope = cdf + t * jnp.exp(-0.5 * t * t) * INV_ROOT_TAU
            slope_ref[rows, :] = (live * slope).astype(BF16)
            total = total + jnp.sum(live * (t * cdf), axis=0, keepdims=True)
        pool_ref[...] = jnp.broadcast_to(total, pool_ref.shape)


def chunk_of(idx, length, pieces, frame_map, weight, chunk, before):
    tile = 256
    whole = pl.BlockSpec((CH, COLS), lambda k, n, m: (0, 0))

    def late(k):
        return jnp.maximum(k - 4, 0)

    return pl.pallas_call(
        functools.partial(chunk_kernel, chunk),
        out_shape=(
            jax.ShapeDtypeStruct((SEQ, VIS), BF16),
            jax.ShapeDtypeStruct((SEQ, HID_HERE), BF16),
            jax.ShapeDtypeStruct((8, HID_HERE), F32),
        ),
        grid_spec=pltpu.PrefetchScalarGridSpec(
            num_scalar_prefetch=2,
            grid=(4 + HID_HERE // tile,),
            in_specs=[whole] * 4
            + [
                pl.BlockSpec((ATT, 512), lambda k, n, m: (0, jnp.minimum(k, 3))),
                pl.BlockSpec((ATT, 128), lambda k, n, m: (0, 16)),
                pl.BlockSpec((VIS, tile), lambda k, n, m: (0, late(k))),
            ]
            + [pl.BlockSpec(memory_space=pl.ANY)] * len(before),
            out_specs=(
                pl.BlockSpec((CH, VIS), lambda k, n, m: (chunk, 0)),
                pl.BlockSpec((CH, tile), lambda k, n, m: (chunk, late(k))),
                pl.BlockSpec((8, tile), lambda k, n, m: (0, late(k))),
            ),
            scratch_shapes=[pltpu.VMEM((CH, ATT), BF16)],
        ),
        input_output_aliases={9: 0, 10: 1} if before else {},
        compiler_params=params(),
        cost_estimate=cost(2 * CH * VIS * (ATT + HID_HERE), 20 << 20, 2 * CH * HID_HERE),
        name="chunk",
    )(idx, length, *pieces, frame_map, frame_map, weight, *before)


def assemble_kernel(z_ref, x_ref, core_ref, *refs):
    o_ref = refs[-1]
    lead = core_ref[0] == 0
    for k in range(4):
        x = x_ref[k]
        col = pl.multiple_of((x // 2) * COLS, COLS)
        for i in range(4):
            mine, other = refs[k][i].astype(F32), refs[4 + k][i].astype(F32)
            pair = [jnp.where(lead, mine, other), jnp.where(lead, other, mine)]
            row = pl.multiple_of((z_ref[i] * 2 + x % 2) * 2 * ROWS, 2 * ROWS)
            o_ref[pl.ds(row, 2 * ROWS), pl.ds(col, COLS)] = jnp.concatenate(pair, axis=0).astype(
                BF16
            )


def assemble(z_order, x_order, core, own, other):
    return pl.pallas_call(
        assemble_kernel,
        out_shape=jax.ShapeDtypeStruct((VIS, HID_HERE), BF16),
        in_specs=[pl.BlockSpec(memory_space=pltpu.SMEM)] * 3
        + [pl.BlockSpec(memory_space=pltpu.VMEM)] * 8,
        compiler_params=pltpu.CompilerParams(vmem_limit_bytes=VMEM_LIMIT),
        cost_estimate=cost(1 << 20, 9 << 20),
        name="assemble",
    )(z_order, x_order, core, *own, *other)


def grad_kernel(core_ref, f_ref, s_ref, keep_ref, send_ref, total):
    for r in range(VIS // 128):
        total[r * 128 : (r + 1) * 128, :] = lax.dot_general(
            f_ref[:, r * 128 : (r + 1) * 128],
            s_ref[...],
            (((0,), (0,)), ((), ())),
            preferred_element_type=F32,
        )
    core = core_ref[0]
    for b in range(8):
        mine = pl.multiple_of((2 * b + core) * ROWS, 8)
        other = pl.multiple_of((2 * b + 1 - core) * ROWS, 8)
        keep_ref[b, 0] = total[pl.ds(mine, ROWS), :].astype(BF16)
        send_ref[b, 0] = total[pl.ds(other, ROWS), :].astype(BF16)


def grad_of(core, frames, slope):
    out = jax.ShapeDtypeStruct((8, 2, ROWS, COLS), BF16)
    spec = pl.BlockSpec((8, 1, ROWS, COLS), lambda j, n: (0, j, 0, 0))
    return pl.pallas_call(
        grad_kernel,
        out_shape=(out, out),
        grid_spec=pltpu.PrefetchScalarGridSpec(
            num_scalar_prefetch=1,
            grid=(2,),
            in_specs=[
                pl.BlockSpec((SEQ, VIS), lambda j, n: (0, 0)),
                pl.BlockSpec((SEQ, COLS), lambda j, n: (0, j)),
            ],
            out_specs=(spec, spec),
            scratch_shapes=[pltpu.VMEM((VIS, COLS), F32)],
        ),
        compiler_params=params(),
        cost_estimate=cost(2 * SEQ * HID_HERE * VIS, 11 << 20),
        name="grad",
    )(core, frames, slope)


def logit_kernel(at_ref, part_ref, fact_ref, hw_ref, lp_ref, lg_ref, scale_ref):
    facts = fact_ref[...]
    lane = lax.broadcasted_iota(jnp.int32, (1, 128), 1)
    line = lane.astype(F32)

    def column(rows, i):
        return jnp.sum(jnp.where(lane == i, rows, 0.0), axis=1, keepdims=True)

    gains, groups = column(facts, 0), column(facts, 1)
    member = (groups == line).astype(F32)
    sums = jnp.sum(member * gains, axis=0, keepdims=True)
    squares = jnp.sum(member * (gains * gains), axis=0, keepdims=True)
    sizes = jnp.maximum(jnp.sum(member, axis=0, keepdims=True), 1.0)
    mean = sums / sizes
    spread = jnp.sqrt(jnp.maximum(squares / sizes - mean * mean, 1.0))
    masks = jnp.where((lane >= 16) & (lane < 24), facts, 0.0)
    count = jnp.maximum(jnp.sum(jnp.sum(masks, axis=1, keepdims=True), axis=0, keepdims=True), 1.0)
    action = lax.broadcasted_iota(jnp.int32, (8, 128), 0)
    bins = lax.broadcasted_iota(jnp.int32, (8, NBINS), 1).astype(F32)
    for c in range(2):
        here = fact_ref[pl.ds(at_ref[c], 1), :]
        own = (column(here, 1) == line).astype(F32)
        advantage = (column(here, 0) - jnp.sum(own * mean, axis=1, keepdims=True)) / jnp.sum(
            own * spread, axis=1, keepdims=True
        )
        rows = jnp.broadcast_to(here, (8, 128))
        act = jnp.sum(jnp.where(lane == action + 8, rows, 0.0), axis=1, keepdims=True)
        mask = jnp.sum(jnp.where(lane == action + 16, rows, 0.0), axis=1, keepdims=True)
        weight = -mask * advantage / count

        logits = (part_ref[0, c] + part_ref[1, c]) + (part_ref[2, c] + part_ref[3, c])
        down = logits - jnp.max(logits, axis=-1, keepdims=True)
        log_all = down - jnp.log(jnp.sum(jnp.exp(down), axis=-1, keepdims=True))
        picked = (bins == act).astype(F32)
        lp = jnp.sum(picked * log_all, axis=-1, keepdims=True)
        lp_ref[c] = jnp.broadcast_to(lp, lp_ref.shape[1:])
        grad = (weight * (picked - jnp.exp(log_all))).astype(BF16)
        lg_ref[c] = grad
        back = lax.dot_general(
            grad, hw_ref[...], (((1,), (1,)), ((), ())), preferred_element_type=F32
        )
        pool = jnp.sum(back, axis=0, keepdims=True) / column(here, 2)
        scale_ref[c] = jnp.broadcast_to(pool, scale_ref.shape[1:])


def logit_parts(at, parts, facts, hw):
    return pl.pallas_call(
        logit_kernel,
        out_shape=(
            jax.ShapeDtypeStruct((2, 8, 128), F32),
            jax.ShapeDtypeStruct((2, 8, NBINS), BF16),
            jax.ShapeDtypeStruct((2, 8, HID_HERE), F32),
        ),
        in_specs=[pl.BlockSpec(memory_space=pltpu.SMEM)]
        + [pl.BlockSpec(memory_space=pltpu.VMEM)] * 3,
        compiler_params=pltpu.CompilerParams(vmem_limit_bytes=VMEM_LIMIT),
        cost_estimate=cost(8 << 20, 1 << 20, 8192),
        name="logit",
    )(at, parts, facts, hw)


def scale_kernel(core_ref, keep_ref, got_ref, scale_ref, head_ref, lg_ref, o_ref):
    core = core_ref[0]
    mine = scale_ref[core][0:1]
    other = scale_ref[1 - core][0:1]
    lower = jnp.concatenate([lg_ref[core].astype(F32), jnp.zeros((8, NBINS), F32)], axis=1)
    for b in range(2):
        for x in range(2):
            cols = slice(x * COLS, (x + 1) * COLS)
            top = (
                keep_ref[b, x].astype(F32) * mine[:, cols]
                + got_ref[b, x].astype(F32) * other[:, cols]
            )
            o_ref[b, x] = jnp.concatenate(
                [top, head_ref[:, cols].astype(F32), lower], axis=0
            ).astype(BF16)


def scaled(core, keep, got, scale, head_input, lgrad):
    spec = pl.BlockSpec((2, 2, ROWS, COLS), lambda i, n: (i, 0, 0, 0))
    return pl.pallas_call(
        scale_kernel,
        out_shape=jax.ShapeDtypeStruct((8, 2, ROWS + 16, COLS), BF16),
        grid_spec=pltpu.PrefetchScalarGridSpec(
            num_scalar_prefetch=1,
            grid=(4,),
            in_specs=[
                spec,
                spec,
                pl.BlockSpec((2, 8, HID_HERE), lambda i, n: (0, 0, 0)),
                pl.BlockSpec((8, HID_HERE), lambda i, n: (0, 0)),
                pl.BlockSpec((2, 8, NBINS), lambda i, n: (0, 0, 0)),
            ],
            out_specs=pl.BlockSpec((2, 2, ROWS + 16, COLS), lambda i, n: (i, 0, 0, 0)),
        ),
        compiler_params=params(),
        cost_estimate=cost(8 << 20, 7 << 20),
        name="scaled",
    )(core, keep, got, scale, head_input, lgrad)


def episode_facts(lengths, actions, action_mask, group_ids, rewards):
    three = jnp.stack([rewards, group_ids.astype(F32), lengths.astype(F32)], axis=1)
    return jnp.concatenate(
        [
            jnp.pad(three, ((0, 0), (0, 5))),
            jnp.pad(actions.astype(F32), ((0, 0), (0, 1))),
            jnp.pad(action_mask.astype(F32), ((0, 0), (0, 105))),
        ],
        axis=1,
    )


def per_device(
    queries,
    keys,
    values,
    lengths,
    frame_map,
    proj_weight,
    head_weight,
    act_embed,
    actions,
    action_mask,
    group_ids,
    rewards,
):
    xh = lax.axis_index("xh")
    y = lax.axis_index("y")
    z = lax.axis_index("z")
    xl = lax.axis_index("xl")
    core = lax.axis_index("c")
    core1 = core.reshape(1)
    length = lax.dynamic_slice_in_dim(lengths, xh, 1)

    got = dealt(pack(queries, keys, values), ("xh", "y"))

    x = xh * 2 + xl
    line = ("xh", "xl")
    row = [proj_weight] + [shifted(proj_weight, "z", by) for by in (1, -1, 2)]
    z_order = (z + jnp.array([0, 3, 1, 2], jnp.int32)) % 4
    block = jnp.stack(row)
    up, down = shifted(block, line, 1), shifted(block, line, -1)
    half = jnp.concatenate([shifted(up[:2], line, 1), shifted(down[2:], line, -1)])
    x_order = (x + jnp.array([0, 3, 1, 2], jnp.int32)) % 4
    own = (block, up, down, half)
    other = [shifted(w, "c", 1) for w in own]
    weight = assemble(z_order, x_order, core1, own, other)

    first = xh == 0
    hw_other, ae_other = shifted(head_weight, "xh", 1), shifted(act_embed, "xh", 1)

    def both(mine, other, axis):
        return jnp.concatenate(
            [jnp.where(first, mine, other), jnp.where(first, other, mine)], axis=axis
        )

    hw = both(head_weight, hw_other, 0)
    embed = jnp.pad(both(act_embed, ae_other, 1), ((0, 1), (0, 0)))

    facts = episode_facts(lengths, actions, action_mask, group_ids, rewards)
    facts = jnp.broadcast_to(facts[None], (16, 2, 128))
    facts = dealt(facts, ("z", "xl", "c"))
    places = (z * 2 + xl) * 4 + xh + 2 * jnp.arange(2, dtype=jnp.int32)

    idx = (y + jnp.array([0, 3, 1, 2], jnp.int32)) % 4
    a0 = attend(got, length, 0, ())
    a1 = attend(got, length, 1, ())
    b0 = shifted(a0, "y", 1)
    c0 = shifted(a0, "y", -1)
    b1 = shifted(a1, "y", 1)
    c1 = shifted(a1, "y", -1)
    d0 = shifted(b0, "y", 1)
    d1 = shifted(c1, "y", -1)

    *done, pool0 = chunk_of(idx, length, (a0, b0, c0, d0), frame_map, weight, 0, ())
    frames, slope, pool1 = chunk_of(
        idx, length, (a1, b1, c1, d1), frame_map, weight, 1, tuple(done)
    )
    pooled = (pool0 + pool1) / length.astype(F32)
    head_input = (pooled + embed).astype(BF16)
    part = jnp.dot(head_input, hw, preferred_element_type=F32)
    parts = dealt(jnp.broadcast_to(part[None], (8, 8, NBINS)), ("y", "c"))
    keep, send = grad_of(core1, frames, slope)
    arrived = shifted(send, "c", 1)

    logprob, lgrad, scale = logit_parts(
        places, parts.reshape(4, 2, 8, NBINS), facts.reshape(32, 128), hw
    )
    summed = scaled(core1, keep, arrived, scale, head_input, lgrad)
    dealt_out = dealt(summed.reshape(16, ROWS + 16, COLS), ("z", "xl", "xh"))
    grad_proj = jnp.sum(dealt_out[:, :ROWS].astype(F32), axis=0).astype(BF16)

    own_head = dealt_out[:, ROWS:]
    other_head = shifted(own_head, "c", 1)
    heads = jnp.stack([own_head, other_head])
    lefts = heads[:, :, :8].reshape(256, COLS)
    rights = heads[:, :, 8:, :NBINS].reshape(256, NBINS)
    grad_head = lax.dot_general(
        lefts, rights, (((0,), (0,)), ((), ())), preferred_element_type=F32
    ).astype(BF16)

    lp_mine = lax.dynamic_index_in_dim(logprob[:, :7, 0], core, 0)
    lp_other = shifted(lp_mine, "xh", 1)
    logprobs = both(lp_mine, lp_other, 0)
    return logprobs, grad_proj, grad_head


def solution(mesh):
    fine = Mesh(mesh.devices.reshape(2, 4, 4, 2, 2), ("xh", "y", "z", "xl", "c"))
    cp, grp = ("xh", "y"), ("z", "xl", "c")
    in_specs = (
        P(grp, cp, None),
        P(grp, cp, None),
        P(grp, cp, None),
        P(grp),
        P(),
        P(grp, cp),
        P(cp, None),
        P(None, cp),
        P(grp, None),
        P(grp, None),
        P(grp),
        P(grp),
    )
    out_specs = (P(grp, None), P(grp, cp), P(cp, None))
    return jax.shard_map(
        per_device, mesh=fine, in_specs=in_specs, out_specs=out_specs, check_vma=False
    )
```

```python
import functools
import math

import jax
import jax.numpy as jnp
from jax import lax
from jax.experimental import pallas as pl
from jax.experimental.pallas import tpu as pltpu
from jax.sharding import Mesh
from jax.sharding import PartitionSpec as P


F32, BF16 = jnp.float32, jnp.bfloat16
HD = 128
HEADS_HERE = 4
COLS = 512
ATT = 2048
VIS = 2176
ROWS = 136
HID_HERE = 1024
SEQ = 1024
CHUNKS = 2
CH = SEQ // CHUNKS
NBINS = 256
SQRT_HALF = 0.7071067811865476
INV_ROOT_TAU = 0.3989422804014327
NEG_LARGE = -1e30
EXP2_SCALE = math.log2(math.e) / math.sqrt(HD)
VMEM_LIMIT = 67043328
SMALL = 14 * 1024 * 1024
VMEM = pl.BlockSpec(memory_space=pltpu.VMEM)
SMEM = pl.BlockSpec(memory_space=pltpu.SMEM)
ANY = pl.BlockSpec(memory_space=pl.ANY)
HBM = pl.BlockSpec(memory_space=pltpu.HBM)


def params(limit=VMEM_LIMIT):
    return pltpu.CompilerParams(dimension_semantics=("arbitrary",), vmem_limit_bytes=limit)


def local(limit=SMALL):
    return pltpu.CompilerParams(vmem_limit_bytes=limit)


def cost(flops, nbytes, trans=0):
    return pl.CostEstimate(flops=flops, bytes_accessed=nbytes, transcendentals=trans)


def shifted(x, axis, by):
    count = lax.axis_size(axis)
    return lax.ppermute(x, axis, [(i, (i + by) % count) for i in range(count)])


def across(x, by):
    pairs = [(2 * i + c, 2 * ((i + by) % 4) + 1 - c) for i in range(4) for c in range(2)]
    return lax.ppermute(x, ("y", "c"), pairs)


def dealt(x, axes):
    return lax.all_to_all(x, axes, 0, 0, tiled=True)


def pack_kernel(q_ref, k_ref, v_ref, o_ref):
    for i, ref in enumerate((q_ref, k_ref, v_ref)):
        for j in range(2):
            o_ref[j, i] = ref[0, :, j * COLS : (j + 1) * COLS]


def pack(q, k, v):
    spec = pl.BlockSpec((1, 128, 2 * COLS), lambda i: (i // 2, 0, i % 2))
    return pl.pallas_call(
        pack_kernel,
        out_shape=jax.ShapeDtypeStruct((8, 3, 128, COLS), BF16),
        grid=(4,),
        in_specs=[spec] * 3,
        out_specs=pl.BlockSpec((2, 3, 128, COLS), lambda i: (i, 0, 0, 0)),
        compiler_params=params(),
        cost_estimate=cost(0, 6 << 20),
        name="pack",
    )(q, k, v)


def attend_kernel(chunk, len_ref, got_ref, *rest):
    if chunk == 1:
        map_ref, o_ref, held_ref, sem = rest
        copy = pltpu.make_async_copy(map_ref, held_ref, sem)
        copy.start()
    else:
        o_ref = rest[-1]
    at = lax.broadcasted_iota(jnp.int32, (1, SEQ), 1)
    bias = jnp.where(at < len_ref[0], 0.0, NEG_LARGE)

    @pl.loop(0, HEADS_HERE)
    def _(h):
        lanes = pl.ds(pl.multiple_of(h * HD, HD), HD)
        k = got_ref[:, 1, :, lanes].reshape(SEQ, HD)
        v = got_ref[:, 2, :, lanes].reshape(SEQ, HD)
        for r in range(CH // 256):
            first = chunk * (CH // 128) + 2 * r
            q = got_ref[first : first + 2, 0, :, lanes].reshape(256, HD)
            s = lax.dot_general(q, k, (((1,), (1,)), ((), ())), preferred_element_type=F32)
            s = s + bias
            top = jnp.max(s, axis=-1, keepdims=True)
            p = jnp.exp2((s - top) * EXP2_SCALE)
            total = jnp.sum(p, axis=-1, keepdims=True)
            w = jnp.dot(p.astype(BF16), v, preferred_element_type=F32)
            o_ref[r * 256 : (r + 1) * 256, lanes] = (w / total).astype(BF16)

    if chunk == 1:
        copy.wait()


def attend(got, length, chunk, after):
    out = jax.ShapeDtypeStruct((CH, COLS), BF16)
    held = jax.ShapeDtypeStruct((ATT, VIS), BF16)
    return pl.pallas_call(
        functools.partial(attend_kernel, chunk),
        out_shape=(out, held) if chunk == 1 else out,
        in_specs=[SMEM, VMEM] + ([HBM] if chunk == 1 else [ANY] + [SMEM] * (len(after) - 1)),
        out_specs=(VMEM, VMEM) if chunk == 1 else VMEM,
        scratch_shapes=[pltpu.SemaphoreType.DMA] if chunk == 1 else [],
        compiler_params=local(37 * 1024 * 1024 if chunk == 1 else SMALL),
        cost_estimate=cost(4 * CH * SEQ * COLS, 3 << 20, 4 * CH * SEQ),
        name="attend",
    )(length, got, *after)


TILE = 256


def chunk_kernel(chunk, idx_ref, len_ref, a_ref, b_ref, c_ref, d_ref, fm_ref, w_ref, *rest):
    full, act = rest[-2:]
    rest = rest[:-2]
    if chunk == 0:
        o_ref, slope_ref, pool_ref = rest
    else:
        pool0_ref, ae_ref, ae_other_ref, hw_ref, hw_other_ref = rest[:5]
        o_ref, slope_ref, head_ref, part_ref = rest[5:]
    for i, ref in enumerate((a_ref, b_ref, c_ref, d_ref)):
        full[:, pl.ds(pl.multiple_of(idx_ref[i] * COLS, COLS), COLS)] = ref[...]

    @pl.loop(0, 3)
    def _(n):
        lanes = pl.ds(pl.multiple_of(n * 512, 512), 512)
        o_ref[:, lanes] = jnp.dot(
            full[...], fm_ref[:, lanes], preferred_element_type=F32
        ).astype(BF16)

    o_ref[:, 1536:] = jnp.dot(
        full[...], fm_ref[:, 1536:], preferred_element_type=F32
    ).astype(BF16)

    at = lax.broadcasted_iota(jnp.int32, (CH, 1), 0) + chunk * CH
    live = (at < len_ref[0]).astype(F32)
    tiles = HID_HERE // TILE
    pools = []
    for j in range(tiles + 1):
        if j < tiles:
            act[j % 2] = jnp.dot(
                o_ref[...], w_ref[:, j * TILE : (j + 1) * TILE], preferred_element_type=F32
            )
        if j > 0:
            t = act[(j - 1) % 2]
            cdf = 0.5 * (1.0 + lax.erf(t * SQRT_HALF))
            slope = cdf + t * jnp.exp(-0.5 * t * t) * INV_ROOT_TAU
            slope_ref[:, (j - 1) * TILE : j * TILE] = (live * slope).astype(BF16)
            pools.append(jnp.sum(live * (t * cdf), axis=0, keepdims=True))
    pool = jnp.concatenate(pools, axis=1)
    if chunk == 0:
        pool_ref[...] = jnp.broadcast_to(pool, pool_ref.shape)
        return
    pool_row = (pool + pool0_ref[0:1, :]) / len_ref[0].astype(F32)
    x = len_ref[1]
    part = jnp.zeros((8, NBINS), F32)
    for side, (e_ref, h_ref) in enumerate(((ae_ref, hw_ref), (ae_other_ref, hw_other_ref))):
        embed = jnp.concatenate([e_ref[...], jnp.zeros((1, COLS), F32)], axis=0)
        low, high = pool_row[:, :COLS], pool_row[:, COLS:]
        mine = jnp.where((x == 0) == (side == 0), low, high)
        head = (mine + embed).astype(BF16)
        place = x if side == 0 else 1 - x
        head_ref[:, pl.ds(pl.multiple_of(place * COLS, COLS), COLS)] = head
        part = part + jnp.dot(head, h_ref[...], preferred_element_type=F32)
    part_ref[...] = part


def chunk_of(idx, where, pieces, frame_map, weight, chunk, more):
    shapes = [
        jax.ShapeDtypeStruct((CH, VIS), BF16),
        jax.ShapeDtypeStruct((CH, HID_HERE), BF16),
    ]
    if chunk == 0:
        shapes += [jax.ShapeDtypeStruct((8, HID_HERE), F32)]
    else:
        shapes += [
            jax.ShapeDtypeStruct((8, HID_HERE), BF16),
            jax.ShapeDtypeStruct((8, NBINS), F32),
        ]
    return pl.pallas_call(
        functools.partial(chunk_kernel, chunk),
        out_shape=tuple(shapes),
        in_specs=[SMEM, SMEM] + [VMEM] * (6 + len(more)),
        out_specs=tuple([VMEM] * len(shapes)),
        scratch_shapes=[pltpu.VMEM((CH, ATT), BF16), pltpu.VMEM((2, CH, TILE), F32)],
        compiler_params=local(),
        cost_estimate=cost(2 * CH * VIS * (ATT + HID_HERE), 20 << 20, 2 * CH * HID_HERE),
        name="chunk",
    )(idx, where, *pieces, frame_map, weight, *more)


def assemble_kernel(z_ref, x_ref, core_ref, *refs):
    o_ref = refs[-1]
    lead = core_ref[0] == 0
    for k in range(4):
        x = x_ref[k]
        col = pl.multiple_of((x // 2) * COLS, COLS)
        for i in range(4):
            mine, other = refs[k][i].astype(F32), refs[4 + k][i].astype(F32)
            pair = [jnp.where(lead, mine, other), jnp.where(lead, other, mine)]
            row = pl.multiple_of((z_ref[i] * 2 + x % 2) * 2 * ROWS, 2 * ROWS)
            o_ref[pl.ds(row, 2 * ROWS), pl.ds(col, COLS)] = jnp.concatenate(pair, axis=0).astype(
                BF16
            )


def assemble(z_order, x_order, core, own, other):
    return pl.pallas_call(
        assemble_kernel,
        out_shape=jax.ShapeDtypeStruct((VIS, HID_HERE), BF16),
        in_specs=[SMEM] * 3 + [VMEM] * 8,
        out_specs=VMEM,
        compiler_params=local(),
        cost_estimate=cost(1 << 20, 9 << 20),
        name="assemble",
    )(z_order, x_order, core, *own, *other)


def grad_kernel(core_ref, f0_ref, s0_ref, f1_ref, s1_ref, keep_ref, send_ref, total):
    core = core_ref[0]

    @pl.loop(0, 2)
    def _(x):
        lanes = pl.ds(pl.multiple_of(x * COLS, COLS), COLS)
        for r in range(VIS // 128):
            rows = slice(r * 128, (r + 1) * 128)
            total[rows, :] = sum(
                lax.dot_general(
                    f[:, rows], s[:, lanes], (((0,), (0,)), ((), ())), preferred_element_type=F32
                )
                for f, s in ((f0_ref, s0_ref), (f1_ref, s1_ref))
            )
        for b in range(8):
            mine = pl.multiple_of((2 * b + core) * ROWS, 8)
            other = pl.multiple_of((2 * b + 1 - core) * ROWS, 8)
            keep_ref[b, x] = total[pl.ds(mine, ROWS), :].astype(BF16)
            send_ref[b, x] = total[pl.ds(other, ROWS), :].astype(BF16)


def grad_of(core, *parts):
    out = jax.ShapeDtypeStruct((8, 2, ROWS, COLS), BF16)
    return pl.pallas_call(
        grad_kernel,
        out_shape=(out, out),
        in_specs=[SMEM] + [VMEM] * 4,
        out_specs=(VMEM, VMEM),
        scratch_shapes=[pltpu.VMEM((VIS, COLS), F32)],
        compiler_params=local(),
        cost_estimate=cost(2 * SEQ * HID_HERE * VIS, 11 << 20),
        name="grad",
    )(core, *parts)


def logit_kernel(at_ref, *refs):
    parts, refs = refs[:8], refs[8:]
    near_ref, far_ref, hw_ref, other_ref, lp_ref, lg_ref, scale_ref = refs
    facts = jnp.concatenate([near_ref[...], far_ref[...]], axis=0)
    lane = lax.broadcasted_iota(jnp.int32, (1, 128), 1)
    line = lane.astype(F32)

    def column(rows, i):
        return jnp.sum(jnp.where(lane == i, rows, 0.0), axis=1, keepdims=True)

    gains, groups = column(facts, 0), column(facts, 1)
    member = (groups == line).astype(F32)
    sums = jnp.sum(member * gains, axis=0, keepdims=True)
    squares = jnp.sum(member * (gains * gains), axis=0, keepdims=True)
    sizes = jnp.maximum(jnp.sum(member, axis=0, keepdims=True), 1.0)
    mean = sums / sizes
    spread = jnp.sqrt(jnp.maximum(squares / sizes - mean * mean, 1.0))
    masks = jnp.where((lane >= 16) & (lane < 24), facts, 0.0)
    count = jnp.maximum(jnp.sum(jnp.sum(masks, axis=1, keepdims=True), axis=0, keepdims=True), 1.0)
    action = lax.broadcasted_iota(jnp.int32, (8, 128), 0)
    bins = lax.broadcasted_iota(jnp.int32, (8, NBINS), 1).astype(F32)
    for side in range(2):
        c = at_ref[0] if side == 0 else 1 - at_ref[0]
        here = near_ref[pl.ds(at_ref[1] + 2 * side, 1), :]
        own = (column(here, 1) == line).astype(F32)
        advantage = (column(here, 0) - jnp.sum(own * mean, axis=1, keepdims=True)) / jnp.sum(
            own * spread, axis=1, keepdims=True
        )
        rows = jnp.broadcast_to(here, (8, 128))
        act = jnp.sum(jnp.where(lane == action + 8, rows, 0.0), axis=1, keepdims=True)
        mask = jnp.sum(jnp.where(lane == action + 16, rows, 0.0), axis=1, keepdims=True)
        weight = -mask * advantage / count

        own4 = [ref[...] for ref in parts[4 * side : 4 * side + 4]]
        logits = (own4[0] + own4[1]) + (own4[2] + own4[3])
        down = logits - jnp.max(logits, axis=-1, keepdims=True)
        log_all = down - jnp.log(jnp.sum(jnp.exp(down), axis=-1, keepdims=True))
        picked = (bins == act).astype(F32)
        lp = jnp.sum(picked * log_all, axis=-1, keepdims=True)
        lp_ref[c] = jnp.broadcast_to(lp, lp_ref.shape[1:])
        grad = (weight * (picked - jnp.exp(log_all))).astype(BF16)
        lg_ref[c] = grad
        size = column(here, 2)
        for half, ref in enumerate((hw_ref, other_ref)):
            back = lax.dot_general(
                grad, ref[...], (((1,), (1,)), ((), ())), preferred_element_type=F32
            )
            pool = jnp.sum(back, axis=0, keepdims=True) / size
            place = at_ref[1] if half == 0 else 1 - at_ref[1]
            lanes = pl.ds(pl.multiple_of(place * COLS, COLS), COLS)
            scale_ref[c, :, lanes] = jnp.broadcast_to(pool, (8, COLS))


def logit_parts(at, *operands):
    return pl.pallas_call(
        logit_kernel,
        out_shape=(
            jax.ShapeDtypeStruct((2, 8, 128), F32),
            jax.ShapeDtypeStruct((2, 8, NBINS), BF16),
            jax.ShapeDtypeStruct((2, 8, HID_HERE), F32),
        ),
        in_specs=[SMEM] + [VMEM] * 12,
        out_specs=(VMEM, VMEM, VMEM),
        compiler_params=local(),
        cost_estimate=cost(8 << 20, 1 << 20, 8192),
        name="logit",
    )(at, *operands)


def scale_kernel(core_ref, keep_ref, got_ref, scale_ref, head_ref, lg_ref, o_ref):
    core = core_ref[0]
    mine = scale_ref[core][0:1]
    other = scale_ref[1 - core][0:1]
    lower = jnp.concatenate([lg_ref[core].astype(F32), jnp.zeros((8, NBINS), F32)], axis=1)
    for b in range(2):
        for x in range(2):
            cols = slice(x * COLS, (x + 1) * COLS)
            top = (
                keep_ref[b, x].astype(F32) * mine[:, cols]
                + got_ref[b, x].astype(F32) * other[:, cols]
            )
            o_ref[b, x] = jnp.concatenate(
                [top, head_ref[:, cols].astype(F32), lower], axis=0
            ).astype(BF16)


def scaled(core, keep, got, scale, head_input, lgrad):
    spec = pl.BlockSpec((2, 2, ROWS, COLS), lambda i, n: (i, 0, 0, 0))
    return pl.pallas_call(
        scale_kernel,
        out_shape=jax.ShapeDtypeStruct((8, 2, ROWS + 16, COLS), BF16),
        grid_spec=pltpu.PrefetchScalarGridSpec(
            num_scalar_prefetch=1,
            grid=(4,),
            in_specs=[
                spec,
                spec,
                pl.BlockSpec((2, 8, HID_HERE), lambda i, n: (0, 0, 0)),
                pl.BlockSpec((8, HID_HERE), lambda i, n: (0, 0)),
                pl.BlockSpec((2, 8, NBINS), lambda i, n: (0, 0, 0)),
            ],
            out_specs=pl.BlockSpec((2, 2, ROWS + 16, COLS), lambda i, n: (i, 0, 0, 0)),
        ),
        compiler_params=params(limit=SMALL),
        cost_estimate=cost(8 << 20, 7 << 20),
        name="scaled",
    )(core, keep, got, scale, head_input, lgrad)


def episode_facts(lengths, actions, action_mask, group_ids, rewards):
    three = jnp.stack([rewards, group_ids.astype(F32), lengths.astype(F32)], axis=1)
    return jnp.concatenate(
        [
            jnp.pad(three, ((0, 0), (0, 5))),
            jnp.pad(actions.astype(F32), ((0, 0), (0, 1))),
            jnp.pad(action_mask.astype(F32), ((0, 0), (0, 105))),
        ],
        axis=1,
    )


def per_device(
    queries,
    keys,
    values,
    lengths,
    frame_map,
    proj_weight,
    head_weight,
    act_embed,
    actions,
    action_mask,
    group_ids,
    rewards,
):
    xh = lax.axis_index("xh")
    y = lax.axis_index("y")
    z = lax.axis_index("z")
    xl = lax.axis_index("xl")
    core = lax.axis_index("c")
    core1 = core.reshape(1)
    length = lax.dynamic_slice_in_dim(lengths, xh, 1)

    got = dealt(pack(queries, keys, values), ("xh", "y"))

    x = xh * 2 + xl
    line = ("xh", "xl")
    row = [proj_weight] + [shifted(proj_weight, "z", by) for by in (1, -1, 2)]
    z_order = (z + jnp.array([0, 3, 1, 2], jnp.int32)) % 4
    block = jnp.stack(row)
    up, down = shifted(block, line, 1), shifted(block, line, -1)
    half = shifted(up, line, 1)
    x_order = (x + jnp.array([0, 3, 1, 2], jnp.int32)) % 4
    own = (block, up, down, half)
    other = [shifted(w, "c", 1) for w in own]
    weight = assemble(z_order, x_order, core1, own, other)

    first = xh == 0
    hw_other, ae_other = shifted(head_weight, "xh", 1), shifted(act_embed, "xh", 1)

    def both(mine, other, axis):
        return jnp.concatenate(
            [jnp.where(first, mine, other), jnp.where(first, other, mine)], axis=axis
        )

    facts = episode_facts(lengths, actions, action_mask, group_ids, rewards)
    facts = jnp.concatenate([facts, shifted(facts, "c", 1)])
    facts = jnp.concatenate([facts] + [shifted(facts, "z", by) for by in (1, 2, 3)])
    far_facts = shifted(facts, "xl", 1)
    places = jnp.stack([core, xh]).astype(jnp.int32)
    where = jnp.concatenate([length, xh.reshape(1)])
    idx = (y + jnp.array([0, 3, 1, 2], jnp.int32)) % 4
    a0 = attend(got, where, 0, (facts, idx, z_order, x_order, places, core1))
    a1, held_map = attend(got, where, 1, (frame_map,))
    b0 = shifted(a0, "y", 1)
    c0 = shifted(a0, "y", -1)
    b1 = shifted(a1, "y", 1)
    c1 = shifted(a1, "y", -1)
    d0 = shifted(b0, "y", 1)
    d1 = shifted(c1, "y", -1)

    frames0, slope0, pool0 = chunk_of(idx, where, (a0, b0, c0, d0), held_map, weight, 0, ())
    frames1, slope1, head_input, part = chunk_of(
        idx,
        where,
        (a1, b1, c1, d1),
        held_map,
        weight,
        1,
        (pool0, act_embed, ae_other, head_weight, hw_other),
    )
    near = [part] + [shifted(part, "y", by) for by in (2, 1, 3)]
    far = [across(part, by) for by in (0, 2, 1, 3)]
    keep, send = grad_of(core1, frames0, slope0, frames1, slope1)
    arrived = shifted(send, "c", 1)

    logprob, lgrad, scale = logit_parts(
        places, *near, *far, facts, far_facts, head_weight, hw_other
    )
    summed = scaled(core1, keep, arrived, scale, head_input, lgrad)
    dealt_out = dealt(summed.reshape(16, ROWS + 16, COLS), ("z", "xl", "xh"))
    grad_proj = jnp.sum(dealt_out[:, :ROWS].astype(F32), axis=0).astype(BF16)

    own_head = dealt_out[:, ROWS:]
    other_head = shifted(own_head, "c", 1)
    heads = jnp.stack([own_head, other_head])
    lefts = heads[:, :, :8].reshape(256, COLS)
    rights = heads[:, :, 8:, :NBINS].reshape(256, NBINS)
    grad_head = lax.dot_general(
        lefts, rights, (((0,), (0,)), ((), ())), preferred_element_type=F32
    ).astype(BF16)

    lp_mine = lax.dynamic_index_in_dim(logprob[:, :7, 0], core, 0)
    lp_other = shifted(lp_mine, "xh", 1)
    logprobs = both(lp_mine, lp_other, 0)
    return logprobs, grad_proj, grad_head


def solution(mesh):
    fine = Mesh(mesh.devices.reshape(2, 4, 4, 2, 2), ("xh", "y", "z", "xl", "c"))
    cp, grp = ("xh", "y"), ("z", "xl", "c")
    in_specs = (
        P(grp, cp, None),
        P(grp, cp, None),
        P(grp, cp, None),
        P(grp),
        P(),
        P(grp, cp),
        P(cp, None),
        P(None, cp),
        P(grp, None),
        P(grp, None),
        P(grp),
        P(grp),
    )
    out_specs = (P(grp, None), P(grp, cp), P(cp, None))
    return jax.shard_map(
        per_device, mesh=fine, in_specs=in_specs, out_specs=out_specs, check_vma=False
    )
```

```python
import functools
import math

import jax
import jax.numpy as jnp
from jax import lax
from jax.experimental import pallas as pl
from jax.experimental.pallas import tpu as pltpu
from jax.sharding import Mesh
from jax.sharding import PartitionSpec as P


F32, BF16 = jnp.float32, jnp.bfloat16
HD = 128
HEADS_HERE = 4
COLS = 512
ATT = 2048
VIS = 2176
ROWS = 136
HID_HERE = 1024
SEQ = 1024
CHUNKS = 2
CH = SEQ // CHUNKS
NBINS = 256
SQRT_HALF = 0.7071067811865476
INV_ROOT_TAU = 0.3989422804014327
NEG_LARGE = -1e30
EXP2_SCALE = math.log2(math.e) / math.sqrt(HD)
VMEM_LIMIT = 67043328
SMALL = 14 * 1024 * 1024
VMEM = pl.BlockSpec(memory_space=pltpu.VMEM)
SMEM = pl.BlockSpec(memory_space=pltpu.SMEM)
ANY = pl.BlockSpec(memory_space=pl.ANY)
HBM = pl.BlockSpec(memory_space=pltpu.HBM)


def params(limit=VMEM_LIMIT):
    return pltpu.CompilerParams(dimension_semantics=("arbitrary",), vmem_limit_bytes=limit)


def local(limit=SMALL):
    return pltpu.CompilerParams(vmem_limit_bytes=limit)


def cost(flops, nbytes, trans=0):
    return pl.CostEstimate(flops=flops, bytes_accessed=nbytes, transcendentals=trans)


def shifted(x, axis, by):
    count = lax.axis_size(axis)
    return lax.ppermute(x, axis, [(i, (i + by) % count) for i in range(count)])


def dealt(x, axes):
    return lax.all_to_all(x, axes, 0, 0, tiled=True)


def pack_kernel(q_ref, k_ref, v_ref, o_ref):
    for i, ref in enumerate((q_ref, k_ref, v_ref)):
        for j in range(2):
            o_ref[j, i] = ref[0, :, j * COLS : (j + 1) * COLS]


def pack(q, k, v):
    spec = pl.BlockSpec((1, 128, 2 * COLS), lambda i: (i // 2, 0, i % 2))
    return pl.pallas_call(
        pack_kernel,
        out_shape=jax.ShapeDtypeStruct((8, 3, 128, COLS), BF16),
        grid=(4,),
        in_specs=[spec] * 3,
        out_specs=pl.BlockSpec((2, 3, 128, COLS), lambda i: (i, 0, 0, 0)),
        compiler_params=params(),
        cost_estimate=cost(0, 6 << 20),
        name="pack",
    )(q, k, v)


def attend_kernel(chunk, len_ref, got_ref, *rest):
    if chunk == 1:
        map_ref, o_ref, held_ref, sem = rest
        copy = pltpu.make_async_copy(map_ref, held_ref, sem)
        copy.start()
    else:
        o_ref = rest[-1]
    at = lax.broadcasted_iota(jnp.int32, (1, SEQ), 1)
    bias = jnp.where(at < len_ref[0], 0.0, NEG_LARGE)

    @pl.loop(0, HEADS_HERE)
    def _(h):
        lanes = pl.ds(pl.multiple_of(h * HD, HD), HD)
        k = got_ref[:, 1, :, lanes].reshape(SEQ, HD)
        v = got_ref[:, 2, :, lanes].reshape(SEQ, HD)
        for r in range(CH // 256):
            first = chunk * (CH // 128) + 2 * r
            q = got_ref[first : first + 2, 0, :, lanes].reshape(256, HD)
            s = lax.dot_general(q, k, (((1,), (1,)), ((), ())), preferred_element_type=F32)
            s = s + bias
            top = jnp.max(s, axis=-1, keepdims=True)
            p = jnp.exp2((s - top) * EXP2_SCALE)
            total = jnp.sum(p, axis=-1, keepdims=True)
            w = jnp.dot(p.astype(BF16), v, preferred_element_type=F32)
            o_ref[r * 256 : (r + 1) * 256, lanes] = (w / total).astype(BF16)

    if chunk == 1:
        copy.wait()


def attend(got, length, chunk, after):
    out = jax.ShapeDtypeStruct((CH, COLS), BF16)
    held = jax.ShapeDtypeStruct((ATT, VIS), BF16)
    return pl.pallas_call(
        functools.partial(attend_kernel, chunk),
        out_shape=(out, held) if chunk == 1 else out,
        in_specs=[SMEM, VMEM] + ([HBM] if chunk == 1 else [ANY] + [SMEM] * (len(after) - 1)),
        out_specs=(VMEM, VMEM) if chunk == 1 else VMEM,
        scratch_shapes=[pltpu.SemaphoreType.DMA] if chunk == 1 else [],
        compiler_params=local(37 * 1024 * 1024 if chunk == 1 else SMALL),
        cost_estimate=cost(4 * CH * SEQ * COLS, 3 << 20, 4 * CH * SEQ),
        name="attend",
    )(length, got, *after)


TILE = 256


def chunk_kernel(chunk, idx_ref, len_ref, a_ref, b_ref, c_ref, d_ref, fm_ref, w_ref, *rest):
    full, act = rest[-2:]
    rest = rest[:-2]
    if chunk == 0:
        o_ref, slope_ref, pool_ref = rest
    else:
        pool0_ref, ae_ref, ae_other_ref, hw_ref, hw_other_ref = rest[:5]
        o_ref, slope_ref, head_ref, part_ref = rest[5:]
    for i, ref in enumerate((a_ref, b_ref, c_ref, d_ref)):
        full[:, pl.ds(pl.multiple_of(idx_ref[i] * COLS, COLS), COLS)] = ref[...]

    @pl.loop(0, 3)
    def _(n):
        lanes = pl.ds(pl.multiple_of(n * 512, 512), 512)
        o_ref[:, lanes] = jnp.dot(
            full[...], fm_ref[:, lanes], preferred_element_type=F32
        ).astype(BF16)

    o_ref[:, 1536:] = jnp.dot(
        full[...], fm_ref[:, 1536:], preferred_element_type=F32
    ).astype(BF16)

    at = lax.broadcasted_iota(jnp.int32, (CH, 1), 0) + chunk * CH
    live = (at < len_ref[0]).astype(F32)
    tiles = HID_HERE // TILE
    pools = []
    for j in range(tiles + 1):
        if j < tiles:
            act[j % 2] = jnp.dot(
                o_ref[...], w_ref[:, j * TILE : (j + 1) * TILE], preferred_element_type=F32
            )
        if j > 0:
            t = act[(j - 1) % 2]
            cdf = 0.5 * (1.0 + lax.erf(t * SQRT_HALF))
            slope = cdf + t * jnp.exp(-0.5 * t * t) * INV_ROOT_TAU
            slope_ref[:, (j - 1) * TILE : j * TILE] = (live * slope).astype(BF16)
            pools.append(jnp.sum(live * (t * cdf), axis=0, keepdims=True))
    pool = jnp.concatenate(pools, axis=1)
    if chunk == 0:
        pool_ref[...] = jnp.broadcast_to(pool, pool_ref.shape)
        return
    pool_row = (pool + pool0_ref[0:1, :]) / len_ref[0].astype(F32)
    x = len_ref[1]
    part = jnp.zeros((8, NBINS), F32)
    for side, (e_ref, h_ref) in enumerate(((ae_ref, hw_ref), (ae_other_ref, hw_other_ref))):
        embed = jnp.concatenate([e_ref[...], jnp.zeros((1, COLS), F32)], axis=0)
        low, high = pool_row[:, :COLS], pool_row[:, COLS:]
        mine = jnp.where((x == 0) == (side == 0), low, high)
        head = (mine + embed).astype(BF16)
        place = x if side == 0 else 1 - x
        head_ref[:, pl.ds(pl.multiple_of(place * COLS, COLS), COLS)] = head
        part = part + jnp.dot(head, h_ref[...], preferred_element_type=F32)
    part_ref[...] = part


def chunk_of(idx, where, pieces, frame_map, weight, chunk, more):
    shapes = [
        jax.ShapeDtypeStruct((CH, VIS), BF16),
        jax.ShapeDtypeStruct((CH, HID_HERE), BF16),
    ]
    if chunk == 0:
        shapes += [jax.ShapeDtypeStruct((8, HID_HERE), F32)]
    else:
        shapes += [
            jax.ShapeDtypeStruct((8, HID_HERE), BF16),
            jax.ShapeDtypeStruct((8, NBINS), F32),
        ]
    return pl.pallas_call(
        functools.partial(chunk_kernel, chunk),
        out_shape=tuple(shapes),
        in_specs=[SMEM, SMEM] + [VMEM] * (6 + len(more)),
        out_specs=tuple([VMEM] * len(shapes)),
        scratch_shapes=[pltpu.VMEM((CH, ATT), BF16), pltpu.VMEM((2, CH, TILE), F32)],
        compiler_params=local(),
        cost_estimate=cost(2 * CH * VIS * (ATT + HID_HERE), 20 << 20, 2 * CH * HID_HERE),
        name="chunk",
    )(idx, where, *pieces, frame_map, weight, *more)


def assemble_kernel(z_ref, x_ref, core_ref, *refs):
    o_ref = refs[-1]
    lead = core_ref[0] == 0
    for k in range(4):
        x = x_ref[k]
        col = pl.multiple_of((x // 2) * COLS, COLS)
        for i in range(4):
            ref, j = (k, i) if k < 3 else (3 + i // 2, i % 2)
            mine, other = refs[ref][j].astype(F32), refs[5 + ref][j].astype(F32)
            pair = [jnp.where(lead, mine, other), jnp.where(lead, other, mine)]
            row = pl.multiple_of((z_ref[i] * 2 + x % 2) * 2 * ROWS, 2 * ROWS)
            o_ref[pl.ds(row, 2 * ROWS), pl.ds(col, COLS)] = jnp.concatenate(pair, axis=0).astype(
                BF16
            )


def assemble(z_order, x_order, core, own, other):
    return pl.pallas_call(
        assemble_kernel,
        out_shape=jax.ShapeDtypeStruct((VIS, HID_HERE), BF16),
        in_specs=[SMEM] * 3 + [VMEM] * 10,
        out_specs=VMEM,
        compiler_params=local(),
        cost_estimate=cost(1 << 20, 9 << 20),
        name="assemble",
    )(z_order, x_order, core, *own, *other)


def grad_kernel(half, core_ref, f0_ref, s0_ref, f1_ref, s1_ref, keep_ref, send_ref, total):
    core = core_ref[0]
    lanes = slice(half * COLS, (half + 1) * COLS)
    for r in range(VIS // 128):
        rows = slice(r * 128, (r + 1) * 128)
        total[rows, :] = sum(
            lax.dot_general(
                f[:, rows], s[:, lanes], (((0,), (0,)), ((), ())), preferred_element_type=F32
            )
            for f, s in ((f0_ref, s0_ref), (f1_ref, s1_ref))
        )
    for b in range(8):
        mine = pl.multiple_of((2 * b + core) * ROWS, 8)
        other = pl.multiple_of((2 * b + 1 - core) * ROWS, 8)
        keep_ref[b] = total[pl.ds(mine, ROWS), :].astype(BF16)
        send_ref[b] = total[pl.ds(other, ROWS), :].astype(BF16)


def grad_of(half, core, *parts):
    out = jax.ShapeDtypeStruct((8, ROWS, COLS), BF16)
    return pl.pallas_call(
        functools.partial(grad_kernel, half),
        out_shape=(out, out),
        in_specs=[SMEM] + [VMEM] * 4,
        out_specs=(VMEM, VMEM),
        scratch_shapes=[pltpu.VMEM((VIS, COLS), F32)],
        compiler_params=local(),
        cost_estimate=cost(SEQ * HID_HERE * VIS, 6 << 20),
        name="grad",
    )(core, *parts)


def logit_kernel(at_ref, *refs):
    parts, refs = refs[:4], refs[4:]
    near_ref, far_ref, hw_ref, other_ref, lp_ref, lg_ref, scale_ref = refs
    facts = jnp.concatenate([near_ref[...], far_ref[...]], axis=0)
    lane = lax.broadcasted_iota(jnp.int32, (1, 128), 1)
    line = lane.astype(F32)

    def column(rows, i):
        return jnp.sum(jnp.where(lane == i, rows, 0.0), axis=1, keepdims=True)

    gains, groups = column(facts, 0), column(facts, 1)
    member = (groups == line).astype(F32)
    sums = jnp.sum(member * gains, axis=0, keepdims=True)
    squares = jnp.sum(member * (gains * gains), axis=0, keepdims=True)
    sizes = jnp.maximum(jnp.sum(member, axis=0, keepdims=True), 1.0)
    mean = sums / sizes
    spread = jnp.sqrt(jnp.maximum(squares / sizes - mean * mean, 1.0))
    masks = jnp.where((lane >= 16) & (lane < 24), facts, 0.0)
    count = jnp.maximum(jnp.sum(jnp.sum(masks, axis=1, keepdims=True), axis=0, keepdims=True), 1.0)
    action = lax.broadcasted_iota(jnp.int32, (8, 128), 0)
    bins = lax.broadcasted_iota(jnp.int32, (8, NBINS), 1).astype(F32)
    here = near_ref[pl.ds(at_ref[0], 1), :]
    own = (column(here, 1) == line).astype(F32)
    advantage = (column(here, 0) - jnp.sum(own * mean, axis=1, keepdims=True)) / jnp.sum(
        own * spread, axis=1, keepdims=True
    )
    rows = jnp.broadcast_to(here, (8, 128))
    act = jnp.sum(jnp.where(lane == action + 8, rows, 0.0), axis=1, keepdims=True)
    mask = jnp.sum(jnp.where(lane == action + 16, rows, 0.0), axis=1, keepdims=True)
    weight = -mask * advantage / count

    logits = (parts[0][...] + parts[1][...]) + (parts[2][...] + parts[3][...])
    down = logits - jnp.max(logits, axis=-1, keepdims=True)
    log_all = down - jnp.log(jnp.sum(jnp.exp(down), axis=-1, keepdims=True))
    picked = (bins == act).astype(F32)
    lp = jnp.sum(picked * log_all, axis=-1, keepdims=True)
    lp_ref[...] = jnp.broadcast_to(lp, lp_ref.shape)
    grad = (weight * (picked - jnp.exp(log_all))).astype(BF16)
    lg_ref[...] = grad
    size = column(here, 2)
    for half, ref in enumerate((hw_ref, other_ref)):
        back = lax.dot_general(
            grad, ref[...], (((1,), (1,)), ((), ())), preferred_element_type=F32
        )
        pool = jnp.sum(back, axis=0, keepdims=True) / size
        place = at_ref[0] if half == 0 else 1 - at_ref[0]
        lanes = pl.ds(pl.multiple_of(place * COLS, COLS), COLS)
        scale_ref[:, lanes] = jnp.broadcast_to(pool, (8, COLS))


def logit_parts(at, *operands):
    return pl.pallas_call(
        logit_kernel,
        out_shape=(
            jax.ShapeDtypeStruct((8, 128), F32),
            jax.ShapeDtypeStruct((8, NBINS), BF16),
            jax.ShapeDtypeStruct((8, HID_HERE), F32),
        ),
        in_specs=[SMEM] + [VMEM] * 8,
        out_specs=(VMEM, VMEM, VMEM),
        compiler_params=local(),
        cost_estimate=cost(8 << 20, 1 << 20, 8192),
        name="logit",
    )(at, *operands)


def scale_kernel(keep0, keep1, got0, got1, mine_ref, other_ref, head_ref, lg_ref, o_ref):
    lower = jnp.concatenate([lg_ref[...].astype(F32), jnp.zeros((8, NBINS), F32)], axis=1)
    for x, (keep, got) in enumerate(((keep0, got0), (keep1, got1))):
        cols = slice(x * COLS, (x + 1) * COLS)
        mine, other = mine_ref[0:1, cols], other_ref[0:1, cols]
        head = head_ref[:, cols].astype(F32)
        for b in range(2):
            top = keep[b].astype(F32) * mine + got[b].astype(F32) * other
            o_ref[b, x] = jnp.concatenate([top, head, lower], axis=0).astype(BF16)


def scaled(keeps, gots, mine, other, head_input, lgrad):
    spec = pl.BlockSpec((2, ROWS, COLS), lambda i: (i, 0, 0))

    def whole(columns):
        return pl.BlockSpec((8, columns), lambda i: (0, 0))

    return pl.pallas_call(
        scale_kernel,
        out_shape=jax.ShapeDtypeStruct((8, 2, ROWS + 16, COLS), BF16),
        grid=(4,),
        in_specs=[spec] * 4 + [whole(HID_HERE)] * 3 + [whole(NBINS)],
        out_specs=pl.BlockSpec((2, 2, ROWS + 16, COLS), lambda i: (i, 0, 0, 0)),
        compiler_params=params(limit=SMALL),
        cost_estimate=cost(8 << 20, 7 << 20),
        name="scaled",
    )(*keeps, *gots, mine, other, head_input, lgrad)


def episode_facts(lengths, actions, action_mask, group_ids, rewards):
    three = jnp.stack([rewards, group_ids.astype(F32), lengths.astype(F32)], axis=1)
    return jnp.concatenate(
        [
            jnp.pad(three, ((0, 0), (0, 5))),
            jnp.pad(actions.astype(F32), ((0, 0), (0, 1))),
            jnp.pad(action_mask.astype(F32), ((0, 0), (0, 105))),
        ],
        axis=1,
    )


def per_device(
    queries,
    keys,
    values,
    lengths,
    frame_map,
    proj_weight,
    head_weight,
    act_embed,
    actions,
    action_mask,
    group_ids,
    rewards,
):
    xh = lax.axis_index("xh")
    y = lax.axis_index("y")
    z = lax.axis_index("z")
    xl = lax.axis_index("xl")
    core = lax.axis_index("c")
    core1 = core.reshape(1)
    length = lax.dynamic_slice_in_dim(lengths, xh, 1)

    got = dealt(pack(queries, keys, values), ("xh", "y"))

    x = xh * 2 + xl
    line = ("xh", "xl")
    row = [proj_weight] + [shifted(proj_weight, "z", by) for by in (1, -1, 2)]
    z_order = (z + jnp.array([0, 3, 1, 2], jnp.int32)) % 4
    block = jnp.stack(row)
    up, down = shifted(block, line, 1), shifted(block, line, -1)
    half = (shifted(up[:2], line, 1), shifted(down[2:], line, -1))
    x_order = (x + jnp.array([0, 3, 1, 2], jnp.int32)) % 4
    own = (block, up, down, *half)
    other = [shifted(w, "c", 1) for w in own]
    weight = assemble(z_order, x_order, core1, own, other)

    first = xh == 0
    hw_other, ae_other = shifted(head_weight, "xh", 1), shifted(act_embed, "xh", 1)

    def both(mine, other, axis):
        return jnp.concatenate(
            [jnp.where(first, mine, other), jnp.where(first, other, mine)], axis=axis
        )

    facts = episode_facts(lengths, actions, action_mask, group_ids, rewards)
    facts = jnp.concatenate([facts, shifted(facts, "c", 1)])
    facts = jnp.concatenate([facts] + [shifted(facts, "z", by) for by in (1, 2, 3)])
    far_facts = shifted(facts, "xl", 1)
    places = xh.reshape(1)
    where = jnp.concatenate([length, xh.reshape(1)])
    idx = (y + jnp.array([0, 3, 1, 2], jnp.int32)) % 4
    a0 = attend(got, where, 0, (facts, idx, z_order, x_order, places, core1))
    a1, held_map = attend(got, where, 1, (frame_map,))
    b0 = shifted(a0, "y", 1)
    c0 = shifted(a0, "y", -1)
    b1 = shifted(a1, "y", 1)
    c1 = shifted(a1, "y", -1)
    d0 = shifted(b0, "y", 1)
    d1 = shifted(c1, "y", -1)

    frames0, slope0, pool0 = chunk_of(idx, where, (a0, b0, c0, d0), held_map, weight, 0, ())
    frames1, slope1, head_input, part = chunk_of(
        idx,
        where,
        (a1, b1, c1, d1),
        held_map,
        weight,
        1,
        (pool0, act_embed, ae_other, head_weight, hw_other),
    )
    parts = [part] + [shifted(part, "y", by) for by in (2, 1, 3)]
    done = (frames0, slope0, frames1, slope1)
    keep_a, send_a = grad_of(0, core1, *done)
    got_a = shifted(send_a, "c", 1)
    keep_b, send_b = grad_of(1, core1, *done)
    got_b = shifted(send_b, "c", 1)
    logprob, lgrad, scale = logit_parts(
        places, *parts, facts, far_facts, head_weight, hw_other
    )
    scale_other = shifted(scale, "c", 1)
    summed = scaled((keep_a, keep_b), (got_a, got_b), scale, scale_other, head_input, lgrad)
    dealt_out = dealt(summed.reshape(16, ROWS + 16, COLS), ("z", "xl", "xh"))
    grad_proj = jnp.sum(dealt_out[:, :ROWS].astype(F32), axis=0).astype(BF16)

    own_head = dealt_out[:, ROWS:]
    other_head = shifted(own_head, "c", 1)
    heads = jnp.stack([own_head, other_head])
    lefts = heads[:, :, :8].reshape(256, COLS)
    rights = heads[:, :, 8:, :NBINS].reshape(256, NBINS)
    grad_head = lax.dot_general(
        lefts, rights, (((0,), (0,)), ((), ())), preferred_element_type=F32
    ).astype(BF16)

    lp_mine = logprob[:7, 0][None]
    lp_other = shifted(lp_mine, "xh", 1)
    logprobs = both(lp_mine, lp_other, 0)
    return logprobs, grad_proj, grad_head


def solution(mesh):
    fine = Mesh(mesh.devices.reshape(2, 4, 4, 2, 2), ("xh", "y", "z", "xl", "c"))
    cp, grp = ("xh", "y"), ("z", "xl", "c")
    in_specs = (
        P(grp, cp, None),
        P(grp, cp, None),
        P(grp, cp, None),
        P(grp),
        P(),
        P(grp, cp),
        P(cp, None),
        P(None, cp),
        P(grp, None),
        P(grp, None),
        P(grp),
        P(grp),
    )
    out_specs = (P(grp, None), P(grp, cp), P(cp, None))
    return jax.shard_map(
        per_device, mesh=fine, in_specs=in_specs, out_specs=out_specs, check_vma=False
    )
```

```python
import functools
import math

import jax
import jax.numpy as jnp
from jax import lax
from jax.experimental import pallas as pl
from jax.experimental.pallas import tpu as pltpu
from jax.sharding import Mesh
from jax.sharding import PartitionSpec as P


F32, BF16 = jnp.float32, jnp.bfloat16
HD = 128
HEADS_HERE = 4
COLS = 512
ATT = 2048
VIS = 2176
ROWS = 136
HID_HERE = 1024
SEQ = 1024
CHUNKS = 2
CH = SEQ // CHUNKS
NBINS = 256
SQRT_HALF = 0.7071067811865476
INV_ROOT_TAU = 0.3989422804014327
NEG_LARGE = -1e30
EXP2_SCALE = math.log2(math.e) / math.sqrt(HD)
VMEM_LIMIT = 67043328
SMALL = 14 * 1024 * 1024
VMEM = pl.BlockSpec(memory_space=pltpu.VMEM)
SMEM = pl.BlockSpec(memory_space=pltpu.SMEM)
ANY = pl.BlockSpec(memory_space=pl.ANY)
HBM = pl.BlockSpec(memory_space=pltpu.HBM)


def params(limit=VMEM_LIMIT):
    return pltpu.CompilerParams(dimension_semantics=("arbitrary",), vmem_limit_bytes=limit)


def local(limit=SMALL):
    return pltpu.CompilerParams(vmem_limit_bytes=limit)


def cost(flops, nbytes, trans=0):
    return pl.CostEstimate(flops=flops, bytes_accessed=nbytes, transcendentals=trans)


def shifted(x, axis, by):
    count = lax.axis_size(axis)
    return lax.ppermute(x, axis, [(i, (i + by) % count) for i in range(count)])


def dealt(x, axes):
    return lax.all_to_all(x, axes, 0, 0, tiled=True)


def pack_kernel(place_ref, q_ref, k_ref, v_ref, *rest):
    outs, sems = rest[:8], rest[8]
    copies = []
    for k in range(8):
        xh = lax.rem(place_ref[0] + k // 4, 2)
        cols = pl.ds(pl.multiple_of(lax.rem(place_ref[1] + k % 4, 4) * COLS, COLS), COLS)
        for i, ref in enumerate((q_ref, k_ref, v_ref)):
            copies.append(
                pltpu.make_async_copy(ref.at[xh, :, cols], outs[k].at[i], sems.at[3 * k + i])
            )
    for k in FAR_FIRST:
        for i in range(3):
            copies[3 * k + i].start()
    for copy in copies:
        copy.wait()


FAR_FIRST = (6, 2, 5, 7, 4, 1, 3, 0)


def pack(place, q, k, v):
    return pl.pallas_call(
        pack_kernel,
        out_shape=tuple([jax.ShapeDtypeStruct((3, 128, COLS), BF16)] * 8),
        in_specs=[SMEM, HBM, HBM, HBM],
        out_specs=tuple([VMEM] * 8),
        scratch_shapes=[pltpu.SemaphoreType.DMA((24,))],
        compiler_params=local(61952 * 1024),
        cost_estimate=cost(0, 6 << 20),
        name="pack",
    )(place, q, k, v)


def to_peer(x, k):
    pairs = [
        (i, (i // 4 + k // 4) % 2 * 4 + (i % 4 + k % 4) % 4) for i in range(8)
    ]
    return lax.ppermute(x, ("xh", "y"), pairs)


def attend_kernel(chunk, len_ref, *rest):
    if chunk == 1:
        got_ref, map_ref, o_ref, held_ref, sem = rest
        copy = pltpu.make_async_copy(map_ref, held_ref, sem)
        copy.start()
    else:
        src_ref, pieces = rest[0], rest[1:9]
        o_ref, got_ref = rest[-2:]
        for k in range(8):
            got_ref[src_ref[k]] = pieces[k][...]
    at = lax.broadcasted_iota(jnp.int32, (1, SEQ), 1)
    bias = jnp.where(at < len_ref[0], 0.0, NEG_LARGE)

    @pl.loop(0, HEADS_HERE)
    def _(h):
        lanes = pl.ds(pl.multiple_of(h * HD, HD), HD)
        k = got_ref[:, 1, :, lanes].reshape(SEQ, HD)
        v = got_ref[:, 2, :, lanes].reshape(SEQ, HD)
        for r in range(CH // 256):
            first = chunk * (CH // 128) + 2 * r
            q = got_ref[first : first + 2, 0, :, lanes].reshape(256, HD)
            s = lax.dot_general(q, k, (((1,), (1,)), ((), ())), preferred_element_type=F32)
            s = s + bias
            top = jnp.max(s, axis=-1, keepdims=True)
            p = jnp.exp2((s - top) * EXP2_SCALE)
            total = jnp.sum(p, axis=-1, keepdims=True)
            w = jnp.dot(p.astype(BF16), v, preferred_element_type=F32)
            o_ref[r * 256 : (r + 1) * 256, lanes] = (w / total).astype(BF16)

    if chunk == 1:
        copy.wait()


def attend(chunk, where, *operands):
    out = jax.ShapeDtypeStruct((CH, COLS), BF16)
    if chunk == 0:
        more = jax.ShapeDtypeStruct((8, 3, 128, COLS), BF16)
        specs = [SMEM] + [VMEM] * 8 + [SMEM] * (len(operands) - 9)
    else:
        more = jax.ShapeDtypeStruct((ATT, VIS), BF16)
        specs = [VMEM, HBM]
    return pl.pallas_call(
        functools.partial(attend_kernel, chunk),
        out_shape=(out, more),
        in_specs=[SMEM] + specs,
        out_specs=(VMEM, VMEM),
        scratch_shapes=[pltpu.SemaphoreType.DMA] if chunk == 1 else [],
        compiler_params=local(37 * 1024 * 1024 if chunk == 1 else SMALL),
        cost_estimate=cost(4 * CH * SEQ * COLS, 3 << 20, 4 * CH * SEQ),
        name="attend",
    )(where, *operands)


TILE = 256


def chunk_kernel(chunk, idx_ref, len_ref, a_ref, b_ref, c_ref, d_ref, fm_ref, w_ref, *rest):
    full, act = rest[-2:]
    rest = rest[:-2]
    if chunk == 0:
        o_ref, slope_ref, pool_ref = rest
    else:
        pool0_ref, ae_ref, ae_other_ref, hw_ref, hw_other_ref = rest[:5]
        o_ref, slope_ref, head_ref, part_ref = rest[5:]
    for i, ref in enumerate((a_ref, b_ref, c_ref, d_ref)):
        full[:, pl.ds(pl.multiple_of(idx_ref[i] * COLS, COLS), COLS)] = ref[...]

    @pl.loop(0, 3)
    def _(n):
        lanes = pl.ds(pl.multiple_of(n * 512, 512), 512)
        o_ref[:, lanes] = jnp.dot(
            full[...], fm_ref[:, lanes], preferred_element_type=F32
        ).astype(BF16)

    o_ref[:, 1536:] = jnp.dot(
        full[...], fm_ref[:, 1536:], preferred_element_type=F32
    ).astype(BF16)

    at = lax.broadcasted_iota(jnp.int32, (CH, 1), 0) + chunk * CH
    live = (at < len_ref[0]).astype(F32)
    tiles = HID_HERE // TILE
    pools = []
    for j in range(tiles + 1):
        if j < tiles:
            act[j % 2] = jnp.dot(
                o_ref[...], w_ref[:, j * TILE : (j + 1) * TILE], preferred_element_type=F32
            )
        if j > 0:
            t = act[(j - 1) % 2]
            cdf = 0.5 * (1.0 + lax.erf(t * SQRT_HALF))
            slope = cdf + t * jnp.exp(-0.5 * t * t) * INV_ROOT_TAU
            slope_ref[:, (j - 1) * TILE : j * TILE] = (live * slope).astype(BF16)
            pools.append(jnp.sum(live * (t * cdf), axis=0, keepdims=True))
    pool = jnp.concatenate(pools, axis=1)
    if chunk == 0:
        pool_ref[...] = jnp.broadcast_to(pool, pool_ref.shape)
        return
    pool_row = (pool + pool0_ref[0:1, :]) / len_ref[0].astype(F32)
    x = len_ref[1]
    part = jnp.zeros((8, NBINS), F32)
    for side, (e_ref, h_ref) in enumerate(((ae_ref, hw_ref), (ae_other_ref, hw_other_ref))):
        embed = jnp.concatenate([e_ref[...], jnp.zeros((1, COLS), F32)], axis=0)
        low, high = pool_row[:, :COLS], pool_row[:, COLS:]
        mine = jnp.where((x == 0) == (side == 0), low, high)
        head = (mine + embed).astype(BF16)
        place = x if side == 0 else 1 - x
        head_ref[:, pl.ds(pl.multiple_of(place * COLS, COLS), COLS)] = head
        part = part + jnp.dot(head, h_ref[...], preferred_element_type=F32)
    part_ref[...] = part


def chunk_of(idx, where, pieces, frame_map, weight, chunk, more):
    shapes = [
        jax.ShapeDtypeStruct((CH, VIS), BF16),
        jax.ShapeDtypeStruct((CH, HID_HERE), BF16),
    ]
    if chunk == 0:
        shapes += [jax.ShapeDtypeStruct((8, HID_HERE), F32)]
    else:
        shapes += [
            jax.ShapeDtypeStruct((8, HID_HERE), BF16),
            jax.ShapeDtypeStruct((8, NBINS), F32),
        ]
    return pl.pallas_call(
        functools.partial(chunk_kernel, chunk),
        out_shape=tuple(shapes),
        in_specs=[SMEM, SMEM] + [VMEM] * (6 + len(more)),
        out_specs=tuple([VMEM] * len(shapes)),
        scratch_shapes=[pltpu.VMEM((CH, ATT), BF16), pltpu.VMEM((2, CH, TILE), F32)],
        compiler_params=local(),
        cost_estimate=cost(2 * CH * VIS * (ATT + HID_HERE), 20 << 20, 2 * CH * HID_HERE),
        name="chunk",
    )(idx, where, *pieces, frame_map, weight, *more)


def assemble_kernel(z_ref, x_ref, core_ref, *refs):
    o_ref, fact_ref = refs[-2:]
    lead = core_ref[0] == 0
    for k in range(4):
        x = x_ref[k]
        col = pl.multiple_of((x // 2) * COLS, COLS)
        for i in range(4):
            ref, j = (k, i) if k < 3 else (3 + i // 2, i % 2)
            mine, other = refs[ref][j].astype(F32), refs[5 + ref][j].astype(F32)
            for n, block in enumerate((mine, other)):
                first = (8 * k + 2 * i + n) * 8
                fact_ref[first : first + 8, :] = block[ROWS:, :128]
            mine, other = mine[:ROWS], other[:ROWS]
            pair = [jnp.where(lead, mine, other), jnp.where(lead, other, mine)]
            row = pl.multiple_of((z_ref[i] * 2 + x % 2) * 2 * ROWS, 2 * ROWS)
            o_ref[pl.ds(row, 2 * ROWS), pl.ds(col, COLS)] = jnp.concatenate(pair, axis=0).astype(
                BF16
            )


def assemble(z_order, x_order, core, own, other):
    return pl.pallas_call(
        assemble_kernel,
        out_shape=(
            jax.ShapeDtypeStruct((VIS, HID_HERE), BF16),
            jax.ShapeDtypeStruct((256, 128), F32),
        ),
        in_specs=[SMEM] * 3 + [VMEM] * 10,
        out_specs=(VMEM, VMEM),
        compiler_params=local(),
        cost_estimate=cost(1 << 20, 9 << 20),
        name="assemble",
    )(z_order, x_order, core, *own, *other)


def grad_kernel(half, core_ref, f0_ref, s0_ref, f1_ref, s1_ref, keep_ref, send_ref, total):
    core = core_ref[0]
    lanes = slice(half * COLS, (half + 1) * COLS)
    for r in range(VIS // 128):
        rows = slice(r * 128, (r + 1) * 128)
        total[rows, :] = sum(
            lax.dot_general(
                f[:, rows], s[:, lanes], (((0,), (0,)), ((), ())), preferred_element_type=F32
            )
            for f, s in ((f0_ref, s0_ref), (f1_ref, s1_ref))
        )
    for b in range(8):
        mine = pl.multiple_of((2 * b + core) * ROWS, 8)
        other = pl.multiple_of((2 * b + 1 - core) * ROWS, 8)
        keep_ref[b] = total[pl.ds(mine, ROWS), :].astype(BF16)
        send_ref[b] = total[pl.ds(other, ROWS), :].astype(BF16)


def grad_of(half, core, *parts):
    out = jax.ShapeDtypeStruct((8, ROWS, COLS), BF16)
    return pl.pallas_call(
        functools.partial(grad_kernel, half),
        out_shape=(out, out),
        in_specs=[SMEM] + [VMEM] * 4,
        out_specs=(VMEM, VMEM),
        scratch_shapes=[pltpu.VMEM((VIS, COLS), F32)],
        compiler_params=local(),
        cost_estimate=cost(SEQ * HID_HERE * VIS, 6 << 20),
        name="grad",
    )(core, *parts)


def logit_kernel(at_ref, *refs):
    parts, refs = refs[:4], refs[4:]
    fact_ref, hw_ref, other_ref, lp_ref, lg_ref, scale_ref = refs
    facts = fact_ref[...]
    lane = lax.broadcasted_iota(jnp.int32, (1, 128), 1)
    line = lane.astype(F32)

    def column(rows, i):
        return jnp.sum(jnp.where(lane == i, rows, 0.0), axis=1, keepdims=True)

    gains = column(facts, 0) + column(facts, 1) + column(facts, 2)
    groups, valid = column(facts, 3), column(facts, 6)
    member = (groups == line).astype(F32) * (0.5 * valid)
    sums = jnp.sum(member * gains, axis=0, keepdims=True)
    squares = jnp.sum(member * (gains * gains), axis=0, keepdims=True)
    sizes = jnp.maximum(jnp.sum(member, axis=0, keepdims=True), 1.0)
    mean = sums / sizes
    spread = jnp.sqrt(jnp.maximum(squares / sizes - mean * mean, 1.0))
    masks = jnp.where((lane >= 16) & (lane < 24), facts, 0.0)
    count = 0.5 * jnp.sum(jnp.sum(masks, axis=1, keepdims=True), axis=0, keepdims=True)
    count = jnp.maximum(count, 1.0)
    action = lax.broadcasted_iota(jnp.int32, (8, 128), 0)
    bins = lax.broadcasted_iota(jnp.int32, (8, NBINS), 1).astype(F32)
    here = fact_ref[pl.ds(at_ref[0], 1), :]
    own = (column(here, 3) == line).astype(F32)
    gain = column(here, 0) + column(here, 1) + column(here, 2)
    advantage = (gain - jnp.sum(own * mean, axis=1, keepdims=True)) / jnp.sum(
        own * spread, axis=1, keepdims=True
    )
    rows = jnp.broadcast_to(here, (8, 128))
    act = jnp.sum(jnp.where(lane == action + 8, rows, 0.0), axis=1, keepdims=True)
    mask = jnp.sum(jnp.where(lane == action + 16, rows, 0.0), axis=1, keepdims=True)
    weight = -mask * advantage / count

    logits = (parts[0][...] + parts[1][...]) + (parts[2][...] + parts[3][...])
    down = logits - jnp.max(logits, axis=-1, keepdims=True)
    log_all = down - jnp.log(jnp.sum(jnp.exp(down), axis=-1, keepdims=True))
    picked = (bins == act).astype(F32)
    lp = jnp.sum(picked * log_all, axis=-1, keepdims=True)
    lp_ref[...] = jnp.broadcast_to(lp, lp_ref.shape)
    grad = (weight * (picked - jnp.exp(log_all))).astype(BF16)
    lg_ref[...] = grad
    size = column(here, 4) * 64.0 + column(here, 5)
    for half, ref in enumerate((hw_ref, other_ref)):
        back = lax.dot_general(
            grad, ref[...], (((1,), (1,)), ((), ())), preferred_element_type=F32
        )
        pool = jnp.sum(back, axis=0, keepdims=True) / size
        place = at_ref[0] if half == 0 else 1 - at_ref[0]
        lanes = pl.ds(pl.multiple_of(place * COLS, COLS), COLS)
        scale_ref[:, lanes] = jnp.broadcast_to(pool, (8, COLS))


def logit_parts(at, *operands):
    return pl.pallas_call(
        logit_kernel,
        out_shape=(
            jax.ShapeDtypeStruct((8, 128), F32),
            jax.ShapeDtypeStruct((8, NBINS), BF16),
            jax.ShapeDtypeStruct((8, HID_HERE), F32),
        ),
        in_specs=[SMEM] + [VMEM] * 7,
        out_specs=(VMEM, VMEM, VMEM),
        compiler_params=local(),
        cost_estimate=cost(8 << 20, 1 << 20, 8192),
        name="logit",
    )(at, *operands)


def scale_kernel(keep0, keep1, got0, got1, mine_ref, other_ref, head_ref, lg_ref, o_ref):
    lower = jnp.concatenate([lg_ref[...].astype(F32), jnp.zeros((8, NBINS), F32)], axis=1)
    for x, (keep, got) in enumerate(((keep0, got0), (keep1, got1))):
        cols = slice(x * COLS, (x + 1) * COLS)
        mine, other = mine_ref[0:1, cols], other_ref[0:1, cols]
        head = head_ref[:, cols].astype(F32)
        for b in range(2):
            top = keep[b].astype(F32) * mine + got[b].astype(F32) * other
            o_ref[b, x] = jnp.concatenate([top, head, lower], axis=0).astype(BF16)


def scaled(keeps, gots, mine, other, head_input, lgrad):
    spec = pl.BlockSpec((2, ROWS, COLS), lambda i: (i, 0, 0))

    def whole(columns):
        return pl.BlockSpec((8, columns), lambda i: (0, 0))

    return pl.pallas_call(
        scale_kernel,
        out_shape=jax.ShapeDtypeStruct((8, 2, ROWS + 16, COLS), BF16),
        grid=(4,),
        in_specs=[spec] * 4 + [whole(HID_HERE)] * 3 + [whole(NBINS)],
        out_specs=pl.BlockSpec((2, 2, ROWS + 16, COLS), lambda i: (i, 0, 0, 0)),
        compiler_params=params(limit=SMALL),
        cost_estimate=cost(8 << 20, 7 << 20),
        name="scaled",
    )(*keeps, *gots, mine, other, head_input, lgrad)


def episode_facts(lengths, actions, action_mask, group_ids, rewards):
    high = lax.reduce_precision(rewards, 8, 7)
    middle = lax.reduce_precision(rewards - high, 8, 7)
    low = lax.reduce_precision((rewards - high) - middle, 8, 7)
    columns = [high, middle, low, group_ids, lengths // 64, lengths % 64, jnp.ones((2,), F32)]
    wide = jnp.concatenate(
        [
            jnp.pad(jnp.stack([c.astype(F32) for c in columns], axis=1), ((0, 0), (0, 1))),
            jnp.pad(actions.astype(F32), ((0, 0), (0, 1))),
            jnp.pad(action_mask.astype(F32), ((0, 0), (0, COLS - 23))),
        ],
        axis=1,
    )
    return jnp.pad(wide, ((0, 6), (0, 0))).astype(BF16)


def per_device(
    queries,
    keys,
    values,
    lengths,
    frame_map,
    proj_weight,
    head_weight,
    act_embed,
    actions,
    action_mask,
    group_ids,
    rewards,
):
    xh = lax.axis_index("xh")
    y = lax.axis_index("y")
    z = lax.axis_index("z")
    xl = lax.axis_index("xl")
    core = lax.axis_index("c")
    core1 = core.reshape(1)
    length = lax.dynamic_slice_in_dim(lengths, xh, 1)

    place = jnp.stack([xh, y]).astype(jnp.int32)
    blocks = pack(place, queries, keys, values)
    got = {k: to_peer(blocks[k], k) for k in FAR_FIRST if k}
    got = [blocks[0]] + [got[k] for k in range(1, 8)]
    steps = jnp.arange(8, dtype=jnp.int32)
    source = (xh + steps // 4) % 2 * 4 + (y + 4 - steps % 4) % 4

    x = xh * 2 + xl
    line = ("xh", "xl")
    shard = jnp.concatenate(
        [proj_weight, episode_facts(lengths, actions, action_mask, group_ids, rewards)]
    )
    row = [shard] + [shifted(shard, "z", by) for by in (1, -1, 2)]
    z_order = (z + jnp.array([0, 3, 1, 2], jnp.int32)) % 4
    block = jnp.stack(row)
    up, down = shifted(block, line, 1), shifted(block, line, -1)
    half = (shifted(up[:2], line, 1), shifted(down[2:], line, -1))
    x_order = (x + jnp.array([0, 3, 1, 2], jnp.int32)) % 4
    own = (block, up, down, *half)
    other = [shifted(w, "c", 1) for w in own]
    weight, facts = assemble(z_order, x_order, core1, own, other)

    first = xh == 0
    hw_other, ae_other = shifted(head_weight, "xh", 1), shifted(act_embed, "xh", 1)

    def both(mine, other, axis):
        return jnp.concatenate(
            [jnp.where(first, mine, other), jnp.where(first, other, mine)], axis=axis
        )

    places = xh.reshape(1)
    where = jnp.concatenate([length, xh.reshape(1)])
    idx = (y + jnp.array([0, 3, 1, 2], jnp.int32)) % 4
    a0, got = attend(
        0, where, source, *got, idx, z_order, x_order, places, core1
    )
    a1, held_map = attend(1, where, got, frame_map)
    b0 = shifted(a0, "y", 1)
    c0 = shifted(a0, "y", -1)
    b1 = shifted(a1, "y", 1)
    c1 = shifted(a1, "y", -1)
    d0 = shifted(b0, "y", 1)
    d1 = shifted(c1, "y", -1)

    frames0, slope0, pool0 = chunk_of(idx, where, (a0, b0, c0, d0), held_map, weight, 0, ())
    frames1, slope1, head_input, part = chunk_of(
        idx,
        where,
        (a1, b1, c1, d1),
        held_map,
        weight,
        1,
        (pool0, act_embed, ae_other, head_weight, hw_other),
    )
    parts = [part] + [shifted(part, "y", by) for by in (2, 1, 3)]
    done = (frames0, slope0, frames1, slope1)
    keep_a, send_a = grad_of(0, core1, *done)
    got_a = shifted(send_a, "c", 1)
    keep_b, send_b = grad_of(1, core1, *done)
    got_b = shifted(send_b, "c", 1)
    logprob, lgrad, scale = logit_parts(
        places, *parts, facts, head_weight, hw_other
    )
    scale_other = shifted(scale, "c", 1)
    summed = scaled((keep_a, keep_b), (got_a, got_b), scale, scale_other, head_input, lgrad)
    dealt_out = dealt(summed.reshape(16, ROWS + 16, COLS), ("z", "xl", "xh"))
    grad_proj = jnp.sum(dealt_out[:, :ROWS].astype(F32), axis=0).astype(BF16)

    own_head = dealt_out[:, ROWS:]
    other_head = shifted(own_head, "c", 1)
    heads = jnp.stack([own_head, other_head])
    lefts = heads[:, :, :8].reshape(256, COLS)
    rights = heads[:, :, 8:, :NBINS].reshape(256, NBINS)
    grad_head = lax.dot_general(
        lefts, rights, (((0,), (0,)), ((), ())), preferred_element_type=F32
    ).astype(BF16)

    lp_mine = logprob[:7, 0][None]
    lp_other = shifted(lp_mine, "xh", 1)
    logprobs = both(lp_mine, lp_other, 0)
    return logprobs, grad_proj, grad_head


def solution(mesh):
    fine = Mesh(mesh.devices.reshape(2, 4, 4, 2, 2), ("xh", "y", "z", "xl", "c"))
    cp, grp = ("xh", "y"), ("z", "xl", "c")
    in_specs = (
        P(grp, cp, None),
        P(grp, cp, None),
        P(grp, cp, None),
        P(grp),
        P(),
        P(grp, cp),
        P(cp, None),
        P(None, cp),
        P(grp, None),
        P(grp, None),
        P(grp),
        P(grp),
    )
    out_specs = (P(grp, None), P(grp, cp), P(cp, None))
    return jax.shard_map(
        per_device, mesh=fine, in_specs=in_specs, out_specs=out_specs, check_vma=False
    )
```
